128 devices in a mesh: ctx: 16 (over x, z), head: 8 (over y, core).
Axes of the slice: x: 4, y: 4, z: 4, core: 2. Of those that a mesh axis runs over, the one named last changes fastest.
Arguments:
- queries: bfloat16 [8192, 8192], P(('ctx', 'head')), may hold values from -5 to 5
- keys: bfloat16 [8192, 1024], P(('ctx', 'head')), may hold values from -5 to 5
- values: bfloat16 [8192, 1024], P(('ctx', 'head')), may hold values from -6 to 6
- vert_blocks: int32 [8, 8], P('head'), may hold values from 0 to 47, as said below
Outputs:
- attended: bfloat16 [8192, 8192], P(('ctx', 'head'))
The draws below stay inside these ranges and needn't reach their ends.
Inputs may be any that keep to these rules, and one draw needn't show every extreme that they name: `vert_blocks`: each row names 8 different blocks in rising order; the first is always block 0; the block (6144) // 128 - 1 appears in row 0.
All inputs are finite; a program needn't handle non-finite values.
Results may differ from the reference program's by a relative error of at most 0.0043.
Values may be sent and summed in bfloat16 or wider, within the bound.
A program may use at most 128 MiB of HBM per device.

```python
import math
import jax
import jax.numpy as jnp
from jax import lax

H = 64
KVH = 8
DH = 128
BAND = 2048
VW = 128
NVB = 8
TOKENS = 8192
NV = 1024
QBLK = 512


def draw_keys(key, part):
    base = jax.random.fold_in(key, 11)
    field = jnp.clip(jax.random.normal(base, (TOKENS, KVH * DH), jnp.float32), -5.0, 5.0)
    return field.astype(jnp.bfloat16)


def draw_queries(key, part):
    base = jax.random.fold_in(key, 13)
    field = jnp.clip(jax.random.normal(base, (TOKENS, H * DH), jnp.float32), -5.0, 5.0)
    return field.astype(jnp.bfloat16)


def draw_vert_blocks(key, part):
    count = (TOKENS - BAND) // VW

    def one_head(index):
        order = jax.random.permutation(jax.random.fold_in(key, index + 100), count - 1) + 1
        chosen = jnp.sort(order[:NVB - 1]).astype(jnp.int32)
        return jnp.concatenate([jnp.zeros((1,), jnp.int32), chosen])
    table = jax.vmap(one_head)(jnp.arange(KVH))
    first = table[0]
    has_last = jnp.any(first == count - 1)
    first = jnp.where(has_last, first, first.at[NVB - 1].set(count - 1))
    table = table.at[0].set(first)
    return table.astype(jnp.int32)


def shard_levels(rng, extent, pieces, low, largest):
    level = 1.0
    for dim, blocks in pieces:
        draws = jax.random.uniform(jax.random.fold_in(jax.random.fold_in(rng, 6), dim), (blocks,), jnp.float32, low / len(pieces), largest / len(pieces))
        level = level * jnp.repeat(jnp.exp(draws), extent[dim] // blocks).reshape((-1,) + (1,) * (len(extent) - 1 - dim))
    return level


def bell_draw(stream_key, shape, deviation, reach, split=(), kind=jnp.bfloat16):
    loudness = shard_levels(stream_key, shape, split, -0.22, 0.18) if split else 1.0
    drawn = jax.random.normal(stream_key, shape, jnp.float32) * deviation * loudness
    return jnp.minimum(jnp.maximum(drawn, -reach), reach).astype(kind)


def setup_inputs(seed: int = 0) -> dict:
    key_list = jax.random.split(jax.random.key(seed), 5)
    return {
        "queries": draw_queries(jax.random.fold_in(key_list[4], 71), 0),
        "keys": draw_keys(jax.random.fold_in(key_list[4], 71), 0),
        "values": bell_draw(key_list[2], (TOKENS, KVH * DH), 1.0, 6.0, ((0, 128),)),
        "vert_blocks": draw_vert_blocks(jax.random.fold_in(key_list[4], 71), 0),
    }


def reference(queries, keys, values, vert_blocks):
    per_group = H // KVH
    scale = 1.0 / math.sqrt(DH)
    offsets = jnp.arange(VW, dtype=jnp.int32)
    positions = (vert_blocks[:, :, None] * VW + offsets[None, None, :]).reshape(KVH, NV).astype(jnp.int32)
    head_index = jnp.arange(KVH, dtype=jnp.int32)[:, None]
    keys_three = keys.reshape(TOKENS, KVH, DH)
    values_three = values.reshape(TOKENS, KVH, DH)
    vert_keys = keys_three[positions, head_index].astype(jnp.float32)
    vert_values = values_three[positions, head_index].astype(jnp.float32)
    keys_padded = jnp.pad(keys, ((BAND, 0), (0, 0)))
    values_padded = jnp.pad(values, ((BAND, 0), (0, 0)))

    def one_block(anchor):
        query_block = lax.dynamic_slice_in_dim(queries, anchor, QBLK, 0).reshape(QBLK, KVH, per_group, DH).astype(jnp.float32)
        key_window = lax.dynamic_slice_in_dim(keys_padded, anchor, BAND + QBLK, 0).reshape(BAND + QBLK, KVH, DH).astype(jnp.float32)
        value_window = lax.dynamic_slice_in_dim(values_padded, anchor, BAND + QBLK, 0).reshape(BAND + QBLK, KVH, DH).astype(jnp.float32)
        query_pos = anchor + jnp.arange(QBLK, dtype=jnp.int32)
        key_pos = anchor - BAND + jnp.arange(BAND + QBLK, dtype=jnp.int32)
        spacing = query_pos[:, None] - key_pos[None, :]
        band_mask = (spacing >= 0) & (spacing < BAND) & (key_pos[None, :] >= 0)
        band_scores = jnp.einsum('qgpd,kgd->gpqk', query_block, key_window) * scale
        vert_scores = jnp.einsum('qgpd,gkd->gpqk', query_block, vert_keys) * scale
        vert_mask = positions[:, None, None, :] <= (query_pos - BAND)[None, None, :, None]
        band_scores = jnp.where(band_mask[None, None], band_scores, -jnp.inf)
        vert_scores = jnp.where(vert_mask, vert_scores, -jnp.inf)
        top = jnp.maximum(lax.optimization_barrier(jnp.max(band_scores, axis=-1)), lax.optimization_barrier(jnp.max(vert_scores, axis=-1)))
        band_p = jnp.where(band_mask[None, None], jnp.exp(band_scores - top[..., None]), 0.0)
        vert_p = jnp.where(vert_mask, jnp.exp(vert_scores - top[..., None]), 0.0)
        total = lax.optimization_barrier(jnp.sum(band_p, axis=-1)) + lax.optimization_barrier(jnp.sum(vert_p, axis=-1))
        band_w = lax.optimization_barrier(band_p.astype(jnp.bfloat16)).astype(jnp.float32)
        vert_w = lax.optimization_barrier(vert_p.astype(jnp.bfloat16)).astype(jnp.float32)
        numer = jnp.einsum('gpqk,kgd->qgpd', band_w, value_window) + jnp.einsum('gpqk,gkd->qgpd', vert_w, vert_values)
        result = numer / jnp.transpose(total, (2, 0, 1))[..., None]
        return result.reshape(QBLK, H * DH).astype(jnp.bfloat16)
    starts = jnp.arange(0, TOKENS, QBLK, dtype=jnp.int32)
    blocks = lax.map(one_block, starts)
    return blocks.reshape(TOKENS, H * DH)
```

```python
import functools
import math

import jax
import jax.numpy as jnp
from jax import lax
from jax.experimental import pallas as pl
from jax.experimental.pallas import tpu as pltpu
from jax.sharding import PartitionSpec as P

DH = 128
VW = 128
NVB = 8
NC = 16
NH = 8
ROWS = 64
SLAB = 512
BAND = 2048
HPG = 8
WIDTH = HPG * DH
M = ROWS * HPG
BANDK = BAND + 2 * ROWS
KVROWS = BAND + SLAB + ROWS
NK = BANDK + NVB * VW
KB = 256
NEG = -1e30
SCALE = math.log2(math.e) / math.sqrt(float(DH))

BLOCKS = []
_o = 0
while _o < BANDK:
    _w = min(KB, BANDK - _o)
    BLOCKS.append((0, _o, _w, _o))
    _o += _w
for _b in range(0, NVB * VW, KB):
    BLOCKS.append((1, _b, KB, BANDK + _b))


def kernel(
    q_hbm, k_hbm, v_hbm, vb_ref, out_hbm,
    qb, kv, vt, tb, rb, ch, ob, s_ref, m_ref,
    loc, kvs, kvr, qs, qr, bs, br, rs, rr, gs, gr, os_, or_,
):
    c = lax.axis_index("ctx")
    h = lax.axis_index("head")
    x = c // 4
    z = c % 4
    y = h // 2
    core = h % 2

    def remote(src, dst, ssem, rsem, cc, hh):
        return pltpu.make_async_remote_copy(
            src_ref=src, dst_ref=dst, send_sem=ssem, recv_sem=rsem,
            device_id={"ctx": cc, "head": hh}, device_id_type=pl.DeviceIdType.MESH,
        )

    def drain(ref, sem):
        pltpu.make_async_copy(ref, ref, sem).wait()

    def offset(i):
        j = (i - 1) // 2
        dy = jnp.where(i == 0, 0, jnp.where(i == 7, 0, 1 + 2 * j - 3 * (j // 2)))
        dc = jnp.where(i == 0, 1, jnp.where(i == 7, 0, (i - 1) % 2))
        return dy, dc

    def source(i):
        dy, dc = offset(i)
        return ((y + dy) % 4) * 2 + (core + dc) % 2

    def target(i):
        dy, dc = offset(i)
        return ((y + 4 - dy) % 4) * 2 + (core + 2 - dc) % 2

    def pick(shape, b):
        return jnp.zeros(shape, jnp.int32) + vb_ref[0, b]

    def choose(cases):
        r = jnp.zeros(cases[0][1].shape, jnp.float32)
        for mask, value in cases:
            r = jnp.where(mask, value.astype(jnp.float32), r)
        return r.astype(jnp.bfloat16)

    mine = pl.ds(pl.multiple_of(BAND + h * ROWS, ROWS), ROWS)
    own_k = pltpu.make_async_copy(
        k_hbm.at[:, pl.ds(pl.multiple_of(h * DH, DH), DH)], kv.at[mine, pl.ds(0, DH)], loc.at[0])
    own_v = pltpu.make_async_copy(
        v_hbm.at[:, pl.ds(pl.multiple_of(h * DH, DH), DH)], kv.at[mine, pl.ds(DH, DH)], loc.at[1])
    own_q = pltpu.make_async_copy(
        q_hbm.at[:, pl.ds(pl.multiple_of(h * WIDTH, WIDTH), WIDTH)], qb.at[h], loc.at[2])
    own_k.start()
    own_v.start()
    own_q.start()

    barrier = pltpu.get_barrier_semaphore()
    for d in range(1, NH):
        pl.semaphore_signal(barrier, inc=1, device_id={"ctx": c, "head": (h + d) % NH},
                            device_id_type=pl.DeviceIdType.MESH)
    for d in range(1, NC):
        pl.semaphore_signal(barrier, inc=1, device_id={"ctx": (c + d) % NC, "head": h},
                            device_id_type=pl.DeviceIdType.MESH)
    kv[pl.ds(BAND + SLAB, ROWS), :] = jnp.zeros((ROWS, 2 * DH), jnp.bfloat16)

    @pl.when(c < 4)
    def _():
        vt[...] = jnp.zeros_like(vt)
        for d in range(1, 5):
            @pl.when(c < d)
            def _():
                kv[pl.ds((4 - d) * SLAB, SLAB), :] = jnp.zeros((SLAB, 2 * DH), jnp.bfloat16)

    pl.semaphore_wait(barrier, NH - 1 + NC - 1)

    def kv_copies(i):
        t = target(i)
        return [
            remote(src.at[:, pl.ds(pl.multiple_of(t * DH, DH), DH)],
                   kv.at[mine, pl.ds(n * DH, DH)], kvs.at[t], kvr.at[h], c, t)
            for n, src in enumerate((k_hbm, v_hbm))
        ]

    def q_copy(i):
        t = target(i)
        return remote(q_hbm.at[:, pl.ds(pl.multiple_of(t * WIDTH, WIDTH), WIDTH)],
                      qb.at[h], qs.at[t], qr.at[h], c, t)

    for i in range(7):
        for cp in kv_copies(i):
            cp.start()
    for i in range(7):
        q_copy(i).start()

    own_k.wait()
    own_v.wait()
    for i in range(7):
        s = source(i)
        drain(kv.at[pl.ds(pl.multiple_of(BAND + s * ROWS, ROWS), ROWS), :], kvr.at[s])

    def slab(d):
        return kv.at[pl.ds((4 - d) * SLAB, SLAB), :]

    def hop(n, cond, d_src, d_dst, cc):
        @pl.when(cond)
        def _():
            remote(slab(d_src), slab(d_dst), bs.at[n], br.at[d_dst - 1], cc, h).start()

    def landed(d):
        @pl.when(c >= d)
        def _():
            drain(slab(d), br.at[d - 1])

    row = x * 4

    @pl.when(x < 3)
    def _():
        for b in range(NVB):
            place = pick((VW, 2 * DH), b) - 4 * c
            tb[pl.ds(b * VW, VW), :] = choose(
                [(place == n, kv[pl.ds(BAND + n * VW, VW), :]) for n in range(4)])
        own = pltpu.make_async_copy(tb.at[pl.ds(pl.multiple_of(c * ROWS, ROWS), ROWS), :],
                                    rb.at[c], loc.at[3])
        own.start()
        for d in range(1, NC):
            j = (c + d) % NC
            remote(tb.at[pl.ds(pl.multiple_of(j * ROWS, ROWS), ROWS), :], rb.at[c],
                   rs.at[j], rr.at[c], j, h).start()
        own.wait()

    hop(0, z < 3, 0, 1, c + 1)
    hop(1, z == 0, 0, 3, c + 3)
    hop(2, x < 3, 0, 4, c + 4)

    for s in range(12):
        @pl.when(c != s)
        def _():
            drain(rb.at[s], rr.at[s])
    holder = pick((ROWS, 2 * DH), c // 2)
    ch[...] = choose(
        [((holder >= 4 * s) & (holder < 4 * s + 4), rb[s]) for s in range(12)])
    for d in range(1, NC):
        j = (c + d) % NC

        @pl.when(j >= 4)
        def _():
            remote(ch, vt.at[pl.ds(pl.multiple_of(c * ROWS, ROWS), ROWS), :],
                   gs.at[j], gr.at[c], j, h).start()

    landed(4)
    hop(3, (x > 0) & (z > 0), 4, 3, c - 1)
    hop(4, (x > 0) & (z == 3), 4, 1, c - 3)
    landed(1)
    hop(5, (z == 1) | (z == 2), 1, 2, c + 1)
    landed(3)
    hop(6, (x > 0) & ((z == 1) | (z == 2)), 3, 2, c - 1)
    landed(2)

    @pl.when(c >= 4)
    def _():
        own = pltpu.make_async_copy(ch, vt.at[pl.ds(pl.multiple_of(c * ROWS, ROWS), ROWS), :],
                                    loc.at[4])
        own.start()
        own.wait()
        for s in range(NC):
            @pl.when(c != s)
            def _():
                drain(vt.at[pl.ds(s * ROWS, ROWS), :], gr.at[s])

    ii = lax.broadcasted_iota(jnp.int32, (ROWS, VW), 0)
    jj = lax.broadcasted_iota(jnp.int32, (ROWS, VW), 1)
    missing = jnp.maximum(BAND - c * SLAB, 0)

    def keep(mask, t):
        return jnp.where(mask[None], t.reshape(HPG, ROWS, VW), NEG).reshape(M, VW)

    def load_q(p):
        return jnp.concatenate([qb[p, :, n * DH:(n + 1) * DH] for n in range(HPG)], axis=0)

    def scores(p, q, blk, slot, mx):
        kind, off, w, col = blk
        base = pl.multiple_of(p * ROWS, ROWS)
        k = kv[pl.ds(base + off, w), :DH] if kind == 0 else vt[off:off + w, :DH]
        s = lax.dot_general(q, k, (((1,), (1,)), ((), ())), preferred_element_type=jnp.float32)
        for t in range(w // VW):
            e = s[:, t * VW:(t + 1) * VW]
            o = off + t * VW
            if kind == 0:
                mask = jj >= missing - base - o
                if o == 0:
                    mask = mask & (jj > ii)
                if o + VW == BANDK:
                    mask = mask & (jj <= ii)
            else:
                mask = (jj - ii + pick((ROWS, VW), o // VW) * VW) <= (c * SLAB + p * ROWS - BAND)
            e = keep(mask, e)
            mx = e if mx is None else jnp.maximum(mx, e)
            s_ref[slot, :, col + t * VW:col + (t + 1) * VW] = e
        return mx

    def finish_max(mx, slot):
        m_ref[slot] = jnp.broadcast_to(jnp.max(mx, axis=1, keepdims=True) * SCALE, (M, VW))

    def weigh(p, blk, slot, acc):
        kind, off, w, col = blk
        base = pl.multiple_of(p * ROWS, ROWS)
        v = kv[pl.ds(base + off, w), DH:] if kind == 0 else vt[off:off + w, DH:]
        v = jnp.concatenate([v, jnp.ones((w, DH), jnp.bfloat16)], axis=1)
        m = m_ref[slot]
        e = [jnp.exp2(s_ref[slot, :, col + t * VW:col + (t + 1) * VW] * SCALE - m).astype(jnp.bfloat16)
             for t in range(w // VW)]
        d = jnp.dot(jnp.concatenate(e, axis=1), v, preferred_element_type=jnp.float32)
        return d if acc is None else acc + d

    def out_copy(p):
        return remote(ob.at[p], out_hbm.at[:, pl.ds(pl.multiple_of(h * WIDTH, WIDTH), WIDTH)],
                      os_.at[p], or_.at[h], c, p)

    def stage(i, slot):
        p = source(i)
        n = source(jnp.minimum(i + 1, 7))

        @pl.when(i < 6)
        def _():
            drain(qb.at[n], qr.at[n])

        q = load_q(n)
        acc = mx = None
        for blk in BLOCKS:
            mx = scores(n, q, blk, 1 - slot, mx)
            acc = weigh(p, blk, slot, acc)
        finish_max(mx, 1 - slot)
        o = (acc[:, :DH] / acc[:, DH:]).astype(jnp.bfloat16)
        for t in range(HPG):
            ob[p, :, t * DH:(t + 1) * DH] = o[t * ROWS:(t + 1) * ROWS]

        @pl.when(i < 7)
        def _():
            out_copy(p).start()

    own_q.wait()
    first = source(0)
    drain(qb.at[first], qr.at[first])
    q = load_q(first)
    mx = None
    for blk in BLOCKS:
        mx = scores(first, q, blk, 0, mx)
    finish_max(mx, 0)

    def body(t, carry):
        stage(2 * t, 0)
        stage(2 * t + 1, 1)
        return carry

    lax.fori_loop(0, 4, body, 0)

    own_o = pltpu.make_async_copy(
        ob.at[h], out_hbm.at[:, pl.ds(pl.multiple_of(h * WIDTH, WIDTH), WIDTH)], loc.at[5])
    own_o.start()

    for i in range(7):
        t = target(i)
        for cp in kv_copies(i):
            cp.wait_send()
        q_copy(i).wait_send()
    for n, cond, d in (
        (0, z < 3, 0), (1, z == 0, 0), (2, x < 3, 0), (3, (x > 0) & (z > 0), 4),
        (4, (x > 0) & (z == 3), 4), (5, (z == 1) | (z == 2), 1),
        (6, (x > 0) & ((z == 1) | (z == 2)), 3),
    ):
        @pl.when(cond)
        def _():
            drain(slab(d), bs.at[n])
    for d in range(1, NC):
        j = (c + d) % NC

        @pl.when(x < 3)
        def _():
            drain(rb.at[0], rs.at[j])

        @pl.when(j >= 4)
        def _():
            drain(ch, gs.at[j])
    for i in range(7):
        p = source(i)
        drain(ob.at[p], os_.at[p])
        drain(out_hbm.at[:, pl.ds(pl.multiple_of(p * WIDTH, WIDTH), WIDTH)], or_.at[p])
    own_o.wait()


def per_device(queries, keys, values, vert_blocks):
    anywhere = pl.BlockSpec(memory_space=pl.ANY)
    dma = pltpu.SemaphoreType.DMA
    bf = jnp.bfloat16
    return pl.pallas_call(
        kernel,
        out_shape=jax.ShapeDtypeStruct((ROWS, NH * WIDTH), bf),
        in_specs=[anywhere, anywhere, anywhere, pl.BlockSpec(memory_space=pltpu.SMEM)],
        out_specs=anywhere,
        scratch_shapes=[
            pltpu.VMEM((NH, ROWS, WIDTH), bf),
            pltpu.VMEM((KVROWS, 2 * DH), bf),
            pltpu.VMEM((NVB * VW, 2 * DH), bf),
            pltpu.VMEM((NVB * VW, 2 * DH), bf),
            pltpu.VMEM((12, ROWS, 2 * DH), bf),
            pltpu.VMEM((ROWS, 2 * DH), bf),
            pltpu.VMEM((NH, ROWS, WIDTH), bf),
            pltpu.VMEM((2, M, NK), jnp.float32),
            pltpu.VMEM((2, M, VW), jnp.float32),
            dma((8,)), dma((NH,)), dma((NH,)), dma((NH,)), dma((NH,)),
            dma((8,)), dma((4,)), dma((NC,)), dma((12,)), dma((NC,)), dma((NC,)),
            dma((NH,)), dma((NH,)),
        ],
        compiler_params=pltpu.CompilerParams(
            collective_id=0, has_side_effects=True, vmem_limit_bytes=60 * 2**20),
        name="sparse_attention",
    )(queries, keys, values, vert_blocks)


def solution(mesh):
    placed = (
        P(("ctx", "head"), None),
        P(("ctx", "head"), None),
        P(("ctx", "head"), None),
        P("head", None),
    )
    return jax.shard_map(
        per_device, mesh=mesh, in_specs=placed, out_specs=P(("ctx", "head"), None), check_vma=False
    )
```

```python
import functools
import math

import jax
import jax.numpy as jnp
from jax import lax
from jax.experimental import pallas as pl
from jax.experimental.pallas import tpu as pltpu
from jax.sharding import PartitionSpec as P

DH = 128
VW = 128
NVB = 8
NC = 16
NH = 8
ROWS = 64
SLAB = 512
BAND = 2048
HPG = 8
WIDTH = HPG * DH
M = ROWS * HPG
BANDK = BAND + 2 * ROWS
KVROWS = BAND + SLAB + ROWS
NK = BANDK + NVB * VW
KB = 256
PIECE = 128
NPIECE = SLAB // PIECE
NEG = -1e30
SCALE = math.log2(math.e) / math.sqrt(float(DH))

BLOCKS = []
_o = 0
while _o < BANDK:
    _w = min(KB, BANDK - _o)
    BLOCKS.append((0, _o, _w, _o))
    _o += _w
for _b in range(0, NVB * VW, KB):
    BLOCKS.append((1, _b, KB, BANDK + _b))


def kernel(
    q_hbm, k_hbm, v_hbm, vb_ref, out_hbm,
    qb, kv, vt, tb, rb, ch, ob, s_ref, m_ref, va, vm,
    loc, kvs, kvr, qs, qr, bs, br, rs, rr, gs, gr, os_, or_,
):
    c = lax.axis_index("ctx")
    h = lax.axis_index("head")
    x = c // 4
    z = c % 4
    y = h // 2
    core = h % 2

    def remote(src, dst, ssem, rsem, cc, hh):
        return pltpu.make_async_remote_copy(
            src_ref=src, dst_ref=dst, send_sem=ssem, recv_sem=rsem,
            device_id={"ctx": cc, "head": hh}, device_id_type=pl.DeviceIdType.MESH,
        )

    def drain(ref, sem):
        pltpu.make_async_copy(ref, ref, sem).wait()

    def offset(i):
        j = (i - 1) // 2
        dy = jnp.where(i == 0, 0, jnp.where(i == 7, 0, 1 + 2 * j - 3 * (j // 2)))
        dc = jnp.where(i == 0, 1, jnp.where(i == 7, 0, (i - 1) % 2))
        return dy, dc

    def source(i):
        dy, dc = offset(i)
        return ((y + dy) % 4) * 2 + (core + dc) % 2

    def target(i):
        dy, dc = offset(i)
        return ((y + 4 - dy) % 4) * 2 + (core + 2 - dc) % 2

    def pick(shape, b):
        return jnp.zeros(shape, jnp.int32) + vb_ref[0, b]

    def choose(cases):
        r = jnp.zeros(cases[0][1].shape, jnp.float32)
        for mask, value in cases:
            r = jnp.where(mask, value.astype(jnp.float32), r)
        return r.astype(jnp.bfloat16)

    mine = pl.ds(pl.multiple_of(BAND + h * ROWS, ROWS), ROWS)
    own_k = pltpu.make_async_copy(
        k_hbm.at[:, pl.ds(pl.multiple_of(h * DH, DH), DH)], kv.at[mine, pl.ds(0, DH)], loc.at[0])
    own_v = pltpu.make_async_copy(
        v_hbm.at[:, pl.ds(pl.multiple_of(h * DH, DH), DH)], kv.at[mine, pl.ds(DH, DH)], loc.at[1])
    own_q = pltpu.make_async_copy(
        q_hbm.at[:, pl.ds(pl.multiple_of(h * WIDTH, WIDTH), WIDTH)], qb.at[h], loc.at[2])
    own_k.start()
    own_v.start()
    own_q.start()

    barrier = pltpu.get_barrier_semaphore()
    for d in range(1, NH):
        pl.semaphore_signal(barrier, inc=1, device_id={"ctx": c, "head": (h + d) % NH},
                            device_id_type=pl.DeviceIdType.MESH)
    for d in range(1, NC):
        pl.semaphore_signal(barrier, inc=1, device_id={"ctx": (c + d) % NC, "head": h},
                            device_id_type=pl.DeviceIdType.MESH)
    kv[pl.ds(BAND + SLAB, ROWS), :] = jnp.zeros((ROWS, 2 * DH), jnp.bfloat16)

    @pl.when(c < 4)
    def _():
        vt[...] = jnp.zeros_like(vt)
        for d in range(1, 5):
            @pl.when(c < d)
            def _():
                kv[pl.ds((4 - d) * SLAB, SLAB), :] = jnp.zeros((SLAB, 2 * DH), jnp.bfloat16)

    pl.semaphore_wait(barrier, NH - 1 + NC - 1)

    def kv_copies(i):
        t = target(i)
        return [
            remote(src.at[:, pl.ds(pl.multiple_of(t * DH, DH), DH)],
                   kv.at[mine, pl.ds(n * DH, DH)], kvs.at[t], kvr.at[h], c, t)
            for n, src in enumerate((k_hbm, v_hbm))
        ]

    def q_copy(i):
        t = target(i)
        return remote(q_hbm.at[:, pl.ds(pl.multiple_of(t * WIDTH, WIDTH), WIDTH)],
                      qb.at[h], qs.at[t], qr.at[h], c, t)

    for i in range(7):
        for cp in kv_copies(i):
            cp.start()
    for i in range(7):
        q_copy(i).start()

    own_k.wait()
    own_v.wait()
    for i in range(7):
        s = source(i)
        drain(kv.at[pl.ds(pl.multiple_of(BAND + s * ROWS, ROWS), ROWS), :], kvr.at[s])

    def slab(d):
        return kv.at[pl.ds((4 - d) * SLAB, SLAB), :]

    def piece(d, k):
        return kv.at[pl.ds((4 - d) * SLAB + k * PIECE, PIECE), :]

    def hop(n, cond, d_src, d_dst, cc, k):
        @pl.when(cond)
        def _():
            remote(piece(d_src, k), piece(d_dst, k), bs.at[n], br.at[d_dst - 1, k], cc, h).start()

    def landed(d, k):
        @pl.when(c >= d)
        def _():
            drain(piece(d, k), br.at[d - 1, k])

    middle = (z == 1) | (z == 2)
    back = x > 0

    def table_send():
        @pl.when(x < 3)
        def _():
            for b in range(NVB):
                place = pick((VW, 2 * DH), b) - 4 * c
                tb[pl.ds(b * VW, VW), :] = choose(
                    [(place == n, kv[pl.ds(BAND + n * VW, VW), :]) for n in range(4)])
            own = pltpu.make_async_copy(tb.at[pl.ds(pl.multiple_of(c * ROWS, ROWS), ROWS), :],
                                        rb.at[c], loc.at[3])
            own.start()
            for d in range(1, NC):
                j = (c + d) % NC
                remote(tb.at[pl.ds(pl.multiple_of(j * ROWS, ROWS), ROWS), :], rb.at[c],
                       rs.at[j], rr.at[c], j, h).start()
            own.wait()

    def table_spread():
        for s in range(12):
            @pl.when(c != s)
            def _():
                drain(rb.at[s], rr.at[s])
        holder = pick((ROWS, 2 * DH), c // 2)
        ch[...] = choose(
            [((holder >= 4 * s) & (holder < 4 * s + 4), rb[s]) for s in range(12)])
        for d in range(1, NC):
            j = (c + d) % NC

            @pl.when(j >= 4)
            def _():
                remote(ch, vt.at[pl.ds(pl.multiple_of(c * ROWS, ROWS), ROWS), :],
                       gs.at[j], gr.at[c], j, h).start()

    def table_wait():
        @pl.when(c >= 4)
        def _():
            own = pltpu.make_async_copy(ch, vt.at[pl.ds(pl.multiple_of(c * ROWS, ROWS), ROWS), :],
                                        loc.at[4])
            own.start()
            own.wait()
            for s in range(NC):
                @pl.when(c != s)
                def _():
                    drain(vt.at[pl.ds(s * ROWS, ROWS), :], gr.at[s])

    table_send()
    for k in range(NPIECE):
        hop(2, x < 3, 0, 4, c + 4, k)
        hop(0, z < 3, 0, 1, c + 1, k)
        hop(1, z == 0, 0, 3, c + 3, k)
    table_spread()
    for k in range(NPIECE):
        landed(4, k)
        hop(3, back & (z > 0), 4, 3, c - 1, k)
        hop(4, back & (z == 3), 4, 1, c - 3, k)
    for k in range(NPIECE):
        landed(1, k)
        hop(5, middle, 1, 2, c + 1, k)
    for k in range(NPIECE):
        landed(3, k)
        hop(6, back & middle, 3, 2, c - 1, k)
    table_wait()

    ii = lax.broadcasted_iota(jnp.int32, (ROWS, VW), 0)
    jj = lax.broadcasted_iota(jnp.int32, (ROWS, VW), 1)
    missing = jnp.maximum(BAND - c * SLAB, 0)

    def keep(mask, t):
        return jnp.where(mask[None], t.reshape(HPG, ROWS, VW), NEG).reshape(M, VW)

    def load_q(p):
        return jnp.concatenate([qb[p, :, n * DH:(n + 1) * DH] for n in range(HPG)], axis=0)

    def scores(p, q, blk, slot, mx):
        kind, off, w, col = blk
        base = pl.multiple_of(p * ROWS, ROWS)
        k = kv[pl.ds(base + off, w), :DH] if kind == 0 else vt[off:off + w, :DH]
        s = lax.dot_general(q, k, (((1,), (1,)), ((), ())), preferred_element_type=jnp.float32)
        for t in range(w // VW):
            e = s[:, t * VW:(t + 1) * VW]
            o = off + t * VW
            if kind == 0:
                mask = jj >= missing - base - o
                if o == 0:
                    mask = mask & (jj > ii)
                if o + VW == BANDK:
                    mask = mask & (jj <= ii)
            else:
                mask = (jj - ii + pick((ROWS, VW), o // VW) * VW) <= (c * SLAB + p * ROWS - BAND)
            e = keep(mask, e)
            mx = e if mx is None else jnp.maximum(mx, e)
            s_ref[slot, :, col + t * VW:col + (t + 1) * VW] = e
        return mx

    def row_max(mx):
        return jnp.broadcast_to(jnp.max(mx, axis=1, keepdims=True) * SCALE, (M, VW))

    def weigh(p, blk, slot, acc):
        kind, off, w, col = blk
        base = pl.multiple_of(p * ROWS, ROWS)
        v = kv[pl.ds(base + off, w), DH:] if kind == 0 else vt[off:off + w, DH:]
        v = jnp.concatenate([v, jnp.ones((w, DH), jnp.bfloat16)], axis=1)
        m = m_ref[slot]
        e = [jnp.exp2(s_ref[slot, :, col + t * VW:col + (t + 1) * VW] * SCALE - m).astype(jnp.bfloat16)
             for t in range(w // VW)]
        d = jnp.dot(jnp.concatenate(e, axis=1), v, preferred_element_type=jnp.float32)
        return d if acc is None else acc + d

    def out_copy(p):
        return remote(ob.at[p], out_hbm.at[:, pl.ds(pl.multiple_of(h * WIDTH, WIDTH), WIDTH)],
                      os_.at[p], or_.at[h], c, p)

    def unit_loop(blocks, before, top, after):
        def begin(i):
            before(i)
            return source(i)

        def stage(i, slot):
            p = source(i)
            n = begin(jnp.minimum(i + 1, 7))
            q = load_q(n)
            acc = mx = None
            for blk in blocks:
                mx = scores(n, q, blk, 1 - slot, mx)
                acc = weigh(p, blk, slot, acc)
            after(i, p, slot, acc)
            m_ref[1 - slot] = top(n, row_max(mx))

        n = begin(0)
        q = load_q(n)
        mx = None
        for blk in blocks:
            mx = scores(n, q, blk, 0, mx)
        m_ref[0] = top(n, row_max(mx))

        def body(t, carry):
            stage(2 * t, 0)
            stage(2 * t + 1, 1)
            return carry

        lax.fori_loop(0, 4, body, 0)

    own_q.wait()

    def q_arrived(i):
        @pl.when(i < 7)
        def _():
            n = source(i)
            drain(qb.at[n], qr.at[n])

    def keep_vertical(i, p, slot, acc):
        va[p] = acc
        vm[p] = m_ref[slot]

    @pl.when(c >= 4)
    def _():
        unit_loop([blk for blk in BLOCKS if blk[0] == 1],
                  lambda i: q_arrived(i), lambda n, m: m, keep_vertical)

    @pl.when(c < 4)
    def _():
        va[...] = jnp.zeros_like(va)
        vm[...] = jnp.full_like(vm, NEG)
        for i in range(7):
            q_arrived(i)

    for k in range(NPIECE):
        landed(2, k)

    def finish(i, p, slot, acc):
        f = jnp.exp2(vm[p] - m_ref[slot])
        acc = acc + va[p] * jnp.concatenate([f, f], axis=1)
        o = (acc[:, :DH] / acc[:, DH:]).astype(jnp.bfloat16)
        for t in range(HPG):
            ob[p, :, t * DH:(t + 1) * DH] = o[t * ROWS:(t + 1) * ROWS]

        @pl.when(i < 7)
        def _():
            out_copy(p).start()

    unit_loop([blk for blk in BLOCKS if blk[0] == 0],
              lambda i: None, lambda n, m: jnp.maximum(m, vm[n]), finish)

    own_o = pltpu.make_async_copy(
        ob.at[h], out_hbm.at[:, pl.ds(pl.multiple_of(h * WIDTH, WIDTH), WIDTH)], loc.at[5])
    own_o.start()

    for i in range(7):
        t = target(i)
        for cp in kv_copies(i):
            cp.wait_send()
        q_copy(i).wait_send()
    for n, cond, d in (
        (0, z < 3, 0), (1, z == 0, 0), (2, x < 3, 0), (3, back & (z > 0), 4),
        (4, back & (z == 3), 4), (5, middle, 1), (6, back & middle, 3),
    ):
        @pl.when(cond)
        def _():
            drain(slab(d), bs.at[n])
    for d in range(1, NC):
        j = (c + d) % NC

        @pl.when(x < 3)
        def _():
            drain(rb.at[0], rs.at[j])

        @pl.when(j >= 4)
        def _():
            drain(ch, gs.at[j])
    for i in range(7):
        p = source(i)
        drain(ob.at[p], os_.at[p])
        drain(out_hbm.at[:, pl.ds(pl.multiple_of(p * WIDTH, WIDTH), WIDTH)], or_.at[p])
    own_o.wait()


def per_device(queries, keys, values, vert_blocks):
    anywhere = pl.BlockSpec(memory_space=pl.ANY)
    dma = pltpu.SemaphoreType.DMA
    bf = jnp.bfloat16
    return pl.pallas_call(
        kernel,
        out_shape=jax.ShapeDtypeStruct((ROWS, NH * WIDTH), bf),
        in_specs=[anywhere, anywhere, anywhere, pl.BlockSpec(memory_space=pltpu.SMEM)],
        out_specs=anywhere,
        scratch_shapes=[
            pltpu.VMEM((NH, ROWS, WIDTH), bf),
            pltpu.VMEM((KVROWS, 2 * DH), bf),
            pltpu.VMEM((NVB * VW, 2 * DH), bf),
            pltpu.VMEM((NVB * VW, 2 * DH), bf),
            pltpu.VMEM((12, ROWS, 2 * DH), bf),
            pltpu.VMEM((ROWS, 2 * DH), bf),
            pltpu.VMEM((NH, ROWS, WIDTH), bf),
            pltpu.VMEM((2, M, NK), jnp.float32),
            pltpu.VMEM((2, M, VW), jnp.float32),
            pltpu.VMEM((NH, M, 2 * DH), jnp.float32),
            pltpu.VMEM((NH, M, VW), jnp.float32),
            dma((8,)), dma((NH,)), dma((NH,)), dma((NH,)), dma((NH,)),
            dma((8,)), dma((4, NPIECE)), dma((NC,)), dma((12,)), dma((NC,)), dma((NC,)),
            dma((NH,)), dma((NH,)),
        ],
        compiler_params=pltpu.CompilerParams(
            collective_id=0, has_side_effects=True, vmem_limit_bytes=60 * 2**20),
        name="sparse_attention",
    )(queries, keys, values, vert_blocks)


def solution(mesh):
    placed = (
        P(("ctx", "head"), None),
        P(("ctx", "head"), None),
        P(("ctx", "head"), None),
        P("head", None),
    )
    return jax.shard_map(
        per_device, mesh=mesh, in_specs=placed, out_specs=P(("ctx", "head"), None), check_vma=False
    )
```

```python
import functools
import math

import jax
import jax.numpy as jnp
from jax import lax
from jax.experimental import pallas as pl
from jax.experimental.pallas import tpu as pltpu
from jax.sharding import PartitionSpec as P

DH = 128
VW = 128
NVB = 8
NC = 16
NH = 8
ROWS = 64
SLAB = 512
BAND = 2048
HPG = 8
WIDTH = HPG * DH
M = ROWS * HPG
BANDK = BAND + 2 * ROWS
KVROWS = BAND + SLAB + ROWS
NK = BANDK + NVB * VW
KB = 256
PIECE = 128
NPIECE = SLAB // PIECE
NEG = -1e30
SCALE = math.log2(math.e) / math.sqrt(float(DH))

BLOCKS = []
_o = 0
while _o < BANDK:
    _w = min(KB, BANDK - _o)
    BLOCKS.append((0, _o, _w, _o))
    _o += _w
for _b in range(0, NVB * VW, KB):
    BLOCKS.append((1, _b, KB, BANDK + _b))


def kernel(
    q_hbm, k_hbm, v_hbm, vb_ref, out_hbm,
    qb, kv, vt, tb, rb, ch, raw, ob, s_ref, m_ref, va, vm,
    loc, kvs, kvr, qs, qr, bs, br, ws, wr, fs, fr,
    rs, rr, gs, gr, os_, or_, rdy,
):
    c = lax.axis_index("ctx")
    h = lax.axis_index("head")
    x = c // 4
    z = c % 4
    y = h // 2
    core = h % 2

    def remote(src, dst, ssem, rsem, cc, hh):
        return pltpu.make_async_remote_copy(
            src_ref=src, dst_ref=dst, send_sem=ssem, recv_sem=rsem,
            device_id={"ctx": cc, "head": hh}, device_id_type=pl.DeviceIdType.MESH,
        )

    def drain(ref, sem):
        pltpu.make_async_copy(ref, ref, sem).wait()

    def offset(i):
        r = i % 3
        dy = jnp.where(i < 6, 2 - r + 3 * (r // 2), 0)
        dc = jnp.where(i < 6, i // 3, 7 - i)
        return dy, dc

    def source(i):
        dy, dc = offset(i)
        return ((y + dy) % 4) * 2 + (core + dc) % 2

    def target(i):
        dy, dc = offset(i)
        return ((y + 4 - dy) % 4) * 2 + (core + 2 - dc) % 2

    def pick(shape, b):
        return jnp.zeros(shape, jnp.int32) + vb_ref[0, b]

    def choose(cases):
        r = jnp.zeros(cases[0][1].shape, jnp.float32)
        for mask, value in cases:
            r = jnp.where(mask, value.astype(jnp.float32), r)
        return r.astype(jnp.bfloat16)

    mine = pl.ds(pl.multiple_of(BAND + h * ROWS, ROWS), ROWS)
    own_k = pltpu.make_async_copy(
        k_hbm.at[:, pl.ds(pl.multiple_of(h * DH, DH), DH)], kv.at[mine, pl.ds(0, DH)], loc.at[0])
    own_v = pltpu.make_async_copy(
        v_hbm.at[:, pl.ds(pl.multiple_of(h * DH, DH), DH)], kv.at[mine, pl.ds(DH, DH)], loc.at[1])
    own_q = pltpu.make_async_copy(
        q_hbm.at[:, pl.ds(pl.multiple_of(h * WIDTH, WIDTH), WIDTH)], qb.at[h], loc.at[2])
    own_k.start()
    own_v.start()
    own_q.start()

    barrier = pltpu.get_barrier_semaphore()

    def signal(sem, cc, hh):
        pl.semaphore_signal(sem, inc=1, device_id={"ctx": cc, "head": hh},
                            device_id_type=pl.DeviceIdType.MESH)

    for d in range(1, NH):
        signal(barrier, c, (h + d) % NH)
    place_here = z * 4 + x
    others = [(n, (n % 4) * 4 + n // 4) for n in range(NC)]
    for n, place in others:
        @pl.when(place > place_here)
        def _():
            signal(barrier, n, h)
    kv[pl.ds(BAND + SLAB, ROWS), :] = jnp.zeros((ROWS, 2 * DH), jnp.bfloat16)
    for d in range(1, 5):
        @pl.when(c < d)
        def _():
            kv[pl.ds((4 - d) * SLAB, SLAB), :] = jnp.zeros((SLAB, 2 * DH), jnp.bfloat16)

    pl.semaphore_wait(barrier, NH - 1 + place_here)
    for n, place in others:
        @pl.when(place < place_here)
        def _():
            signal(rdy.at[c], n, h)

    def ready(n):
        @pl.when((n % 4) * 4 + n // 4 > place_here)
        def _():
            pl.semaphore_wait(rdy.at[n], 1)

    def kv_copies(i):
        t = target(i)
        return [
            remote(src.at[:, pl.ds(pl.multiple_of(t * DH, DH), DH)],
                   kv.at[mine, pl.ds(n * DH, DH)], kvs.at[t], kvr.at[h], c, t)
            for n, src in enumerate((k_hbm, v_hbm))
        ]

    def q_copy(i):
        t = target(i)
        return remote(q_hbm.at[:, pl.ds(pl.multiple_of(t * WIDTH, WIDTH), WIDTH)],
                      qb.at[h], qs.at[t], qr.at[h], c, t)

    far = pl.ds(pl.multiple_of(h * ROWS, ROWS), ROWS)

    def raw_copy(n):
        return remote((k_hbm, v_hbm)[n], raw.at[n], ws.at[n], wr.at[n], c + 4, h)

    def far_copies(i):
        t = target(i)
        return [
            remote(raw.at[n, :, pl.ds(pl.multiple_of(t * DH, DH), DH)],
                   kv.at[far, pl.ds(n * DH, DH)], fs.at[t], fr.at[h], c, t)
            for n in range(2)
        ]

    for i in range(7):
        for cp in kv_copies(i):
            cp.start()
    q_copy(6).start()

    @pl.when(x < 3)
    def _():
        pl.semaphore_wait(rdy.at[c + 4], 1)
        for n in range(2):
            raw_copy(n).start()

    own_k.wait()
    own_v.wait()
    for i in range(7):
        s = source(i)
        drain(kv.at[pl.ds(pl.multiple_of(BAND + s * ROWS, ROWS), ROWS), :], kvr.at[s])
    for n in range(NC):
        @pl.when(n != c + 4)
        def _():
            ready(n)

    def slab(d):
        return kv.at[pl.ds((4 - d) * SLAB, SLAB), :]

    def piece(d, k):
        return kv.at[pl.ds((4 - d) * SLAB + k * PIECE, PIECE), :]

    def hop(n, cond, d_src, d_dst, cc, k):
        @pl.when(cond)
        def _():
            remote(piece(d_src, k), piece(d_dst, k), bs.at[n], br.at[d_dst - 1, k], cc, h).start()

    def far_landed(k):
        for e in (2 * k, 2 * k + 1):
            @pl.when((c >= 4) & (h != e))
            def _():
                drain(kv.at[pl.ds(e * ROWS, ROWS), :], fr.at[e])

    def landed(d, k):
        @pl.when(c >= d)
        def _():
            drain(piece(d, k), br.at[d - 1, k])

    middle = (z == 1) | (z == 2)
    back = x > 0

    chunk = pl.ds(pl.multiple_of(c * ROWS, ROWS), ROWS)

    def local(src, dst, sem):
        cp = pltpu.make_async_copy(src, dst, sem)
        cp.start()
        return cp

    def table_send():
        @pl.when(x < 3)
        def _():
            for b in range(NVB):
                place = pick((VW, 2 * DH), b) - 4 * c
                tb[pl.ds(b * VW, VW), :] = choose(
                    [(place == n, kv[pl.ds(BAND + n * VW, VW), :]) for n in range(4)])
            for d in range(1, NC):
                j = (c + d) % NC
                remote(tb.at[pl.ds(pl.multiple_of(j * ROWS, ROWS), ROWS), :], rb.at[c],
                       rs.at[j], rr.at[c], j, h).start()
            local(tb.at[chunk, :], rb.at[c], loc.at[3]).wait()

    def table_spread():
        for s in range(12):
            @pl.when(c != s)
            def _():
                drain(rb.at[s], rr.at[s])
        r = rb[0].astype(jnp.float32)
        for s in range(1, 12):
            r = r + rb[s].astype(jnp.float32)
        ch[...] = r.astype(jnp.bfloat16)
        for d in range(1, NC):
            j = (c + d) % NC

            @pl.when(j >= 4)
            def _():
                remote(ch, vt.at[chunk, :], gs.at[j], gr.at[c], j, h).start()

    def table_wait():
        @pl.when(c >= 4)
        def _():
            local(ch, vt.at[chunk, :], loc.at[4]).wait()
            for s in range(NC):
                @pl.when(c != s)
                def _():
                    drain(vt.at[pl.ds(s * ROWS, ROWS), :], gr.at[s])

    table_send()
    for k in range(NPIECE):
        hop(0, z < 3, 0, 1, c + 1, k)
        hop(1, z == 0, 0, 3, c + 3, k)

    @pl.when(x > 0)
    def _():
        for n in range(2):
            drain(raw.at[n], wr.at[n])
        for i in range(7):
            for cp in far_copies(i):
                cp.start()
        for n in range(2):
            local(raw.at[n, :, pl.ds(pl.multiple_of(h * DH, DH), DH)],
                  kv.at[far, pl.ds(n * DH, DH)], loc.at[6]).wait()

    for i in range(6):
        q_copy(i).start()
    table_spread()
    for k in range(NPIECE):
        far_landed(k)
        hop(3, back & (z > 0), 4, 3, c - 1, k)
        hop(4, back & (z == 3), 4, 1, c - 3, k)
    for k in range(NPIECE):
        landed(1, k)
        hop(5, middle, 1, 2, c + 1, k)
    for k in range(NPIECE):
        landed(3, k)
        hop(6, back & middle, 3, 2, c - 1, k)
    table_wait()

    ii = lax.broadcasted_iota(jnp.int32, (ROWS, VW), 0)
    jj = lax.broadcasted_iota(jnp.int32, (ROWS, VW), 1)
    missing = jnp.maximum(BAND - c * SLAB, 0)

    def keep(mask, t):
        return jnp.where(mask[None], t.reshape(HPG, ROWS, VW), NEG).reshape(M, VW)

    def load_q(p):
        return jnp.concatenate([qb[p, :, n * DH:(n + 1) * DH] for n in range(HPG)], axis=0)

    def scores(p, q, blk, slot, mx):
        kind, off, w, col = blk
        base = pl.multiple_of(p * ROWS, ROWS)
        k = kv[pl.ds(base + off, w), :DH] if kind == 0 else vt[off:off + w, :DH]
        s = lax.dot_general(q, k, (((1,), (1,)), ((), ())), preferred_element_type=jnp.float32)
        for t in range(w // VW):
            e = s[:, t * VW:(t + 1) * VW]
            o = off + t * VW
            if kind == 0:
                mask = jj >= missing - base - o
                if o == 0:
                    mask = mask & (jj > ii)
                if o + VW == BANDK:
                    mask = mask & (jj <= ii)
            else:
                mask = (jj - ii + pick((ROWS, VW), o // VW) * VW) <= (c * SLAB + p * ROWS - BAND)
            e = keep(mask, e)
            mx = e if mx is None else jnp.maximum(mx, e)
            s_ref[slot, :, col + t * VW:col + (t + 1) * VW] = e
        return mx

    def row_max(mx):
        return jnp.broadcast_to(jnp.max(mx, axis=1, keepdims=True) * SCALE, (M, VW))

    def weigh(p, blk, slot, acc):
        kind, off, w, col = blk
        base = pl.multiple_of(p * ROWS, ROWS)
        v = kv[pl.ds(base + off, w), DH:] if kind == 0 else vt[off:off + w, DH:]
        v = jnp.concatenate([v, jnp.ones((w, DH), jnp.bfloat16)], axis=1)
        m = m_ref[slot]
        e = [jnp.exp2(s_ref[slot, :, col + t * VW:col + (t + 1) * VW] * SCALE - m).astype(jnp.bfloat16)
             for t in range(w // VW)]
        d = jnp.dot(jnp.concatenate(e, axis=1), v, preferred_element_type=jnp.float32)
        return d if acc is None else acc + d

    def out_copy(p):
        return remote(ob.at[p], out_hbm.at[:, pl.ds(pl.multiple_of(h * WIDTH, WIDTH), WIDTH)],
                      os_.at[p], or_.at[h], c, p)

    def unit_loop(blocks, before, top, after):
        def begin(i):
            before(i)
            return source(i)

        def stage(i, slot):
            p = source(i)
            n = begin(jnp.minimum(i + 1, 7))
            q = load_q(n)
            acc = mx = None
            for blk in blocks:
                mx = scores(n, q, blk, 1 - slot, mx)
                acc = weigh(p, blk, slot, acc)
            after(i, p, slot, acc)
            m_ref[1 - slot] = top(n, row_max(mx))

        n = begin(0)
        q = load_q(n)
        mx = None
        for blk in blocks:
            mx = scores(n, q, blk, 0, mx)
        m_ref[0] = top(n, row_max(mx))

        def body(t, carry):
            stage(2 * t, 0)
            stage(2 * t + 1, 1)
            return carry

        lax.fori_loop(0, 4, body, 0)

    own_q.wait()

    def q_arrived(i):
        @pl.when(i < 7)
        def _():
            n = source(i)
            drain(qb.at[n], qr.at[n])

    def keep_vertical(i, p, slot, acc):
        va[p] = acc
        vm[p] = m_ref[slot]

    @pl.when(c >= 4)
    def _():
        unit_loop([blk for blk in BLOCKS if blk[0] == 1],
                  lambda i: q_arrived(i), lambda n, m: m, keep_vertical)

    @pl.when(c < 4)
    def _():
        va[...] = jnp.zeros_like(va)
        vm[...] = jnp.full_like(vm, NEG)
        for i in range(7):
            q_arrived(i)

    for k in range(NPIECE):
        landed(2, k)

    def finish(i, p, slot, acc):
        f = jnp.exp2(vm[p] - m_ref[slot])
        acc = acc + va[p] * jnp.concatenate([f, f], axis=1)
        o = (acc[:, :DH] / acc[:, DH:]).astype(jnp.bfloat16)
        for t in range(HPG):
            ob[p, :, t * DH:(t + 1) * DH] = o[t * ROWS:(t + 1) * ROWS]

        @pl.when(i < 7)
        def _():
            out_copy(p).start()

    unit_loop([blk for blk in BLOCKS if blk[0] == 0],
              lambda i: None, lambda n, m: jnp.maximum(m, vm[n]), finish)

    own_o = pltpu.make_async_copy(
        ob.at[h], out_hbm.at[:, pl.ds(pl.multiple_of(h * WIDTH, WIDTH), WIDTH)], loc.at[5])
    own_o.start()

    for i in range(7):
        t = target(i)
        for cp in kv_copies(i):
            cp.wait_send()
        q_copy(i).wait_send()
    for n, cond, d in (
        (0, z < 3, 0), (1, z == 0, 0), (3, back & (z > 0), 4),
        (4, back & (z == 3), 4), (5, middle, 1), (6, back & middle, 3),
    ):
        @pl.when(cond)
        def _():
            drain(slab(d), bs.at[n])

    @pl.when(x < 3)
    def _():
        for n in range(2):
            drain(raw.at[n], ws.at[n])

    @pl.when(x > 0)
    def _():
        for i in range(7):
            for cp in far_copies(i):
                cp.wait_send()

    for d in range(1, NC):
        j = (c + d) % NC

        @pl.when(x < 3)
        def _():
            drain(rb.at[0], rs.at[j])

        @pl.when(j >= 4)
        def _():
            drain(ch, gs.at[j])
    for i in range(7):
        p = source(i)
        drain(ob.at[p], os_.at[p])
        drain(out_hbm.at[:, pl.ds(pl.multiple_of(p * WIDTH, WIDTH), WIDTH)], or_.at[p])
    own_o.wait()


def per_device(queries, keys, values, vert_blocks):
    anywhere = pl.BlockSpec(memory_space=pl.ANY)
    dma = pltpu.SemaphoreType.DMA
    bf = jnp.bfloat16
    return pl.pallas_call(
        kernel,
        out_shape=jax.ShapeDtypeStruct((ROWS, NH * WIDTH), bf),
        in_specs=[anywhere, anywhere, anywhere, pl.BlockSpec(memory_space=pltpu.SMEM)],
        out_specs=anywhere,
        scratch_shapes=[
            pltpu.VMEM((NH, ROWS, WIDTH), bf),
            pltpu.VMEM((KVROWS, 2 * DH), bf),
            pltpu.VMEM((NVB * VW, 2 * DH), bf),
            pltpu.VMEM((NVB * VW, 2 * DH), bf),
            pltpu.VMEM((12, ROWS, 2 * DH), bf),
            pltpu.VMEM((ROWS, 2 * DH), bf),
            pltpu.VMEM((2, ROWS, NH * DH), bf),
            pltpu.VMEM((NH, ROWS, WIDTH), bf),
            pltpu.VMEM((2, M, NK), jnp.float32),
            pltpu.VMEM((2, M, VW), jnp.float32),
            pltpu.VMEM((NH, M, 2 * DH), jnp.float32),
            pltpu.VMEM((NH, M, VW), jnp.float32),
            dma((8,)), dma((NH,)), dma((NH,)), dma((NH,)), dma((NH,)),
            dma((8,)), dma((4, NPIECE)), dma((2,)), dma((2,)), dma((NH,)), dma((NH,)),
            dma((NC,)), dma((12,)), dma((NC,)), dma((NC,)), dma((NH,)), dma((NH,)),
            pltpu.SemaphoreType.REGULAR((NC,)),
        ],
        compiler_params=pltpu.CompilerParams(
            collective_id=0, has_side_effects=True, vmem_limit_bytes=60 * 2**20),
        name="sparse_attention",
    )(queries, keys, values, vert_blocks)


def solution(mesh):
    placed = (
        P(("ctx", "head"), None),
        P(("ctx", "head"), None),
        P(("ctx", "head"), None),
        P("head", None),
    )
    return jax.shard_map(
        per_device, mesh=mesh, in_specs=placed, out_specs=P(("ctx", "head"), None), check_vma=False
    )
```

```python
import functools
import math

import jax
import jax.numpy as jnp
from jax import lax
from jax.experimental import pallas as pl
from jax.experimental.pallas import tpu as pltpu
from jax.sharding import PartitionSpec as P

DH = 128
VW = 128
NVB = 8
NC = 16
NH = 8
ROWS = 64
SLAB = 512
BAND = 2048
HPG = 8
WIDTH = HPG * DH
M = ROWS * HPG
NEARK = SLAB + 2 * ROWS
NEARROWS = 2 * SLAB + ROWS
MIDK = 3 * SLAB
RESTK = MIDK + NVB * VW
KB = 256
PIECE = 128
NPIECE = SLAB // PIECE
QUART = 256
NEG = -1e30
SCALE = math.log2(math.e) / math.sqrt(float(DH))

def cut(kind, size, col):
    return [(kind, o, min(KB, size - o), col + o) for o in range(0, size, KB)]


NEAR = cut(0, NEARK, 0)
REST = cut(1, MIDK, 0) + cut(2, NVB * VW, MIDK)


def kernel(
    q_hbm, k_hbm, v_hbm, vb_ref, out_hbm,
    qb, near, mid, vt, tb, rb, ub, zb, ch, ob, s_ref, m_ref, va, vm,
    loc, kvs, kvr, qs, qr, bs, br,
    sxs, sxr, szs, szr, gzs, gzr, gxs, gxr, os_, or_, rx, rz,
):
    c = lax.axis_index("ctx")
    h = lax.axis_index("head")
    x = c // 4
    z = c % 4
    y = h // 2
    core = h % 2

    def remote(src, dst, ssem, rsem, cc, hh):
        return pltpu.make_async_remote_copy(
            src_ref=src, dst_ref=dst, send_sem=ssem, recv_sem=rsem,
            device_id={"ctx": cc, "head": hh}, device_id_type=pl.DeviceIdType.MESH,
        )

    def drain(ref, sem):
        pltpu.make_async_copy(ref, ref, sem).wait()

    def offset(i):
        r = i % 3
        dy = jnp.where(i < 6, 2 - r + 3 * (r // 2), 0)
        dc = jnp.where(i < 6, i // 3, 7 - i)
        return dy, dc

    def source(i):
        dy, dc = offset(i)
        return ((y + dy) % 4) * 2 + (core + dc) % 2

    def target(i):
        dy, dc = offset(i)
        return ((y + 4 - dy) % 4) * 2 + (core + 2 - dc) % 2

    def pick(shape, b):
        return jnp.zeros(shape, jnp.int32) + vb_ref[0, b]

    def choose(cases):
        r = jnp.zeros(cases[0][1].shape, jnp.float32)
        for mask, value in cases:
            r = jnp.where(mask, value.astype(jnp.float32), r)
        return r.astype(jnp.bfloat16)

    mine = pl.ds(pl.multiple_of(SLAB + h * ROWS, ROWS), ROWS)
    own_k = pltpu.make_async_copy(
        k_hbm.at[:, pl.ds(pl.multiple_of(h * DH, DH), DH)], near.at[mine, pl.ds(0, DH)], loc.at[0])
    own_v = pltpu.make_async_copy(
        v_hbm.at[:, pl.ds(pl.multiple_of(h * DH, DH), DH)], near.at[mine, pl.ds(DH, DH)], loc.at[1])
    own_q = pltpu.make_async_copy(
        q_hbm.at[:, pl.ds(pl.multiple_of(h * WIDTH, WIDTH), WIDTH)], qb.at[h], loc.at[2])
    own_k.start()
    own_v.start()
    own_q.start()

    barrier = pltpu.get_barrier_semaphore()

    def at(xx, zz):
        return xx * 4 + zz

    def signal(sem, cc, hh):
        pl.semaphore_signal(sem, inc=1, device_id={"ctx": cc, "head": hh},
                            device_id_type=pl.DeviceIdType.MESH)

    for d in range(1, NH):
        signal(barrier, c, (h + d) % NH)
    for n in range(1, 4):
        @pl.when(n > x)
        def _():
            signal(barrier, at(n, z), h)

        @pl.when(n > z)
        def _():
            signal(barrier, at(x, n), h)
    near[pl.ds(2 * SLAB, ROWS), :] = jnp.zeros((ROWS, 2 * DH), jnp.bfloat16)

    @pl.when(c < 4)
    def _():
        near[pl.ds(0, SLAB), :] = jnp.zeros((SLAB, 2 * DH), jnp.bfloat16)
        vt[...] = jnp.zeros_like(vt)
        for d in range(1, 4):
            @pl.when(c < d)
            def _():
                mid[pl.ds((3 - d) * SLAB, SLAB), :] = jnp.zeros((SLAB, 2 * DH), jnp.bfloat16)

    pl.semaphore_wait(barrier, NH - 1 + x + z)
    for n in range(3):
        @pl.when(n < x)
        def _():
            signal(rx.at[x], at(n, z), h)

        @pl.when(n < z)
        def _():
            signal(rz.at[z], at(x, n), h)

    def kv_copies(i):
        t = target(i)
        return [
            remote(src.at[:, pl.ds(pl.multiple_of(t * DH, DH), DH)],
                   near.at[mine, pl.ds(n * DH, DH)], kvs.at[t], kvr.at[h], c, t)
            for n, src in enumerate((k_hbm, v_hbm))
        ]

    def q_copy(i):
        t = target(i)
        return remote(q_hbm.at[:, pl.ds(pl.multiple_of(t * WIDTH, WIDTH), WIDTH)],
                      qb.at[h], qs.at[t], qr.at[h], c, t)

    for i in range(7):
        for cp in kv_copies(i):
            cp.start()
    q_copy(6).start()

    for i in range(6):
        q_copy(i).start()
    own_k.wait()
    own_v.wait()
    for i in range(7):
        s = source(i)
        drain(near.at[pl.ds(pl.multiple_of(SLAB + s * ROWS, ROWS), ROWS), :], kvr.at[s])
    for n in range(1, 4):
        @pl.when(n > x)
        def _():
            pl.semaphore_wait(rx.at[n], 1)

        @pl.when(n > z)
        def _():
            pl.semaphore_wait(rz.at[n], 1)

    def part(d, start, rows):
        if d == 0 or d == 4:
            return near.at[pl.ds(start + (SLAB if d == 0 else 0), rows), :]
        return mid.at[pl.ds(start + (3 - d) * SLAB, rows), :]

    def slab(d):
        return part(d, 0, SLAB)

    def piece(d, k):
        return part(d, k * PIECE, PIECE)

    def hop(n, cond, d_src, d_dst, cc, k):
        @pl.when(cond)
        def _():
            remote(piece(d_src, k), piece(d_dst, k), bs.at[n], br.at[d_dst - 1, k], cc, h).start()

    def landed(d, k):
        @pl.when(c >= d)
        def _():
            drain(piece(d, k), br.at[d - 1, k])

    middle = (z == 1) | (z == 2)
    back = x > 0

    quarter = pl.ds(pl.multiple_of(x * QUART, QUART), QUART)
    chunk = pl.ds(pl.multiple_of(x * QUART + z * ROWS, ROWS), ROWS)

    def local(src, dst, sem):
        cp = pltpu.make_async_copy(src, dst, sem)
        cp.start()
        return cp

    def total(parts):
        r = parts[0].astype(jnp.float32)
        for e in parts[1:]:
            r = r + e.astype(jnp.float32)
        return r.astype(jnp.bfloat16)

    def table_add_x():
        @pl.when(x < 3)
        def _():
            for b in range(NVB):
                place = pick((VW, 2 * DH), b) - 4 * c
                tb[pl.ds(b * VW, VW), :] = choose(
                    [(place == n, near[pl.ds(SLAB + n * VW, VW), :]) for n in range(4)])
            for n in range(4):
                @pl.when(n != x)
                def _():
                    remote(tb.at[pl.ds(n * QUART, QUART), :], rb.at[x],
                           sxs.at[n], sxr.at[x], at(n, z), h).start()
            local(tb.at[quarter, :], rb.at[x], loc.at[3]).wait()

    def table_add_z():
        for n in range(3):
            @pl.when(n != x)
            def _():
                drain(rb.at[n], sxr.at[n])
        ub[...] = total([rb[n] for n in range(3)])
        for n in range(4):
            @pl.when(n != z)
            def _():
                remote(ub.at[pl.ds(n * ROWS, ROWS), :], zb.at[z],
                       szs.at[n], szr.at[z], at(x, n), h).start()
        local(ub.at[pl.ds(pl.multiple_of(z * ROWS, ROWS), ROWS), :], zb.at[z], loc.at[3]).wait()

    def table_gather_z():
        for n in range(4):
            @pl.when(n != z)
            def _():
                drain(zb.at[n], szr.at[n])
        ch[...] = total([zb[n] for n in range(4)])
        for n in range(4):
            @pl.when(n != z)
            def _():
                remote(ch, vt.at[chunk, :], gzs.at[n], gzr.at[z], at(x, n), h).start()
        local(ch, vt.at[chunk, :], loc.at[4]).wait()

    def table_gather_x():
        for n in range(4):
            @pl.when(n != z)
            def _():
                drain(ch, gzr.at[n])
        for n in range(1, 4):
            @pl.when(n != x)
            def _():
                remote(vt.at[quarter, :], vt.at[quarter, :],
                       gxs.at[n], gxr.at[x], at(n, z), h).start()

    def table_wait():
        for n in range(4):
            @pl.when((x > 0) & (n != x))
            def _():
                drain(vt.at[pl.ds(n * QUART, QUART), :], gxr.at[n])

    table_add_x()
    for k in range(NPIECE):
        hop(2, x < 3, 0, 4, c + 4, k)
    for k in range(NPIECE):
        hop(0, z < 3, 0, 1, c + 1, k)
        hop(1, z == 0, 0, 3, c + 3, k)
    table_add_z()
    for k in range(NPIECE):
        landed(4, k)
        hop(3, back & (z > 0), 4, 3, c - 1, k)
        hop(4, back & (z == 3), 4, 1, c - 3, k)
    table_gather_z()
    for k in range(NPIECE):
        landed(1, k)
        hop(5, middle, 1, 2, c + 1, k)
    table_gather_x()
    for k in range(NPIECE):
        landed(3, k)
        hop(6, back & middle, 3, 2, c - 1, k)

    ii = lax.broadcasted_iota(jnp.int32, (ROWS, VW), 0)
    jj = lax.broadcasted_iota(jnp.int32, (ROWS, VW), 1)
    missing = (jnp.where(c < 4, SLAB, 0), jnp.maximum(3 - c, 0) * SLAB)

    def keep(mask, t):
        return jnp.where(mask[None], t.reshape(HPG, ROWS, VW), NEG).reshape(M, VW)

    def load_q(p):
        return jnp.concatenate([qb[p, :, n * DH:(n + 1) * DH] for n in range(HPG)], axis=0)

    def load(p, blk, column):
        kind, off, w, _ = blk
        cols = pl.ds(column * DH, DH)
        if kind == 0:
            return near[pl.ds(pl.multiple_of(p * ROWS, ROWS) + off, w), cols]
        return mid[pl.ds(off, w), cols] if kind == 1 else vt[pl.ds(off, w), cols]

    def scores(p, q, blk, slot, mx):
        kind, off, w, col = blk
        k = load(p, blk, 0)
        s = lax.dot_general(q, k, (((1,), (1,)), ((), ())), preferred_element_type=jnp.float32)
        for t in range(w // VW):
            e = s[:, t * VW:(t + 1) * VW]
            o = off + t * VW
            if kind == 0:
                mask = jj >= missing[0] - p * ROWS - o
                if o == 0:
                    mask = mask & (jj > ii)
                if o + VW == NEARK:
                    mask = mask & (jj <= ii)
            elif kind == 1:
                mask = jj >= missing[1] - o
            else:
                mask = (jj - ii + pick((ROWS, VW), o // VW) * VW) <= (c * SLAB + p * ROWS - BAND)
            e = keep(mask, e)
            mx = e if mx is None else jnp.maximum(mx, e)
            s_ref[slot, :, col + t * VW:col + (t + 1) * VW] = e
        return mx

    def row_max(mx):
        return jnp.broadcast_to(jnp.max(mx, axis=1, keepdims=True) * SCALE, (M, VW))

    def weigh(p, blk, slot, acc):
        kind, off, w, col = blk
        v = load(p, blk, 1)
        v = jnp.concatenate([v, jnp.ones((w, DH), jnp.bfloat16)], axis=1)
        m = m_ref[slot]
        e = [jnp.exp2(s_ref[slot, :, col + t * VW:col + (t + 1) * VW] * SCALE - m).astype(jnp.bfloat16)
             for t in range(w // VW)]
        d = jnp.dot(jnp.concatenate(e, axis=1), v, preferred_element_type=jnp.float32)
        return d if acc is None else acc + d

    def out_copy(p):
        return remote(ob.at[p], out_hbm.at[:, pl.ds(pl.multiple_of(h * WIDTH, WIDTH), WIDTH)],
                      os_.at[p], or_.at[h], c, p)

    def unit_loop(blocks, before, top, after):
        def begin(i):
            before(i)
            return source(i)

        def stage(i, slot):
            p = source(i)
            n = begin(jnp.minimum(i + 1, 7))
            q = load_q(n)
            acc = mx = None
            for blk in blocks:
                mx = scores(n, q, blk, 1 - slot, mx)
                acc = weigh(p, blk, slot, acc)
            after(i, p, slot, acc)
            m_ref[1 - slot] = top(n, row_max(mx))

        n = begin(0)
        q = load_q(n)
        mx = None
        for blk in blocks:
            mx = scores(n, q, blk, 0, mx)
        m_ref[0] = top(n, row_max(mx))

        def body(t, carry):
            stage(2 * t, 0)
            stage(2 * t + 1, 1)
            return carry

        lax.fori_loop(0, 4, body, 0)

    own_q.wait()

    def q_arrived(i):
        @pl.when(i < 7)
        def _():
            n = source(i)
            drain(qb.at[n], qr.at[n])

    def keep_near(i, p, slot, acc):
        va[p] = acc
        vm[p] = m_ref[slot]

    unit_loop(NEAR, q_arrived, lambda n, m: m, keep_near)

    for k in range(NPIECE):
        landed(2, k)
    table_wait()

    def finish(i, p, slot, acc):
        f = jnp.exp2(vm[p] - m_ref[slot])
        acc = acc + va[p] * jnp.concatenate([f, f], axis=1)
        o = (acc[:, :DH] / acc[:, DH:]).astype(jnp.bfloat16)
        for t in range(HPG):
            ob[p, :, t * DH:(t + 1) * DH] = o[t * ROWS:(t + 1) * ROWS]

        @pl.when(i < 7)
        def _():
            out_copy(p).start()

    unit_loop(REST, lambda i: None, lambda n, m: jnp.maximum(m, vm[n]), finish)

    own_o = pltpu.make_async_copy(
        ob.at[h], out_hbm.at[:, pl.ds(pl.multiple_of(h * WIDTH, WIDTH), WIDTH)], loc.at[5])
    own_o.start()

    for i in range(7):
        t = target(i)
        for cp in kv_copies(i):
            cp.wait_send()
        q_copy(i).wait_send()
    for n, cond, d in (
        (0, z < 3, 0), (1, z == 0, 0), (2, x < 3, 0), (3, back & (z > 0), 4),
        (4, back & (z == 3), 4), (5, middle, 1), (6, back & middle, 3),
    ):
        @pl.when(cond)
        def _():
            drain(slab(d), bs.at[n])

    for n in range(4):
        @pl.when((x < 3) & (n != x))
        def _():
            drain(rb.at[0], sxs.at[n])

        @pl.when(n != z)
        def _():
            drain(ch, szs.at[n])
            drain(ch, gzs.at[n])

        if n > 0:
            @pl.when(n != x)
            def _():
                drain(rb.at[0], gxs.at[n])
    for i in range(7):
        p = source(i)
        drain(ob.at[p], os_.at[p])
        drain(out_hbm.at[:, pl.ds(pl.multiple_of(p * WIDTH, WIDTH), WIDTH)], or_.at[p])
    own_o.wait()


def per_device(queries, keys, values, vert_blocks):
    anywhere = pl.BlockSpec(memory_space=pl.ANY)
    queries, keys, values, vert_blocks = (
        pltpu.with_memory_space_constraint(e, pltpu.HBM)
        for e in (queries, keys, values, vert_blocks))
    dma = pltpu.SemaphoreType.DMA
    bf = jnp.bfloat16
    return pl.pallas_call(
        kernel,
        out_shape=jax.ShapeDtypeStruct((ROWS, NH * WIDTH), bf),
        in_specs=[anywhere, anywhere, anywhere, pl.BlockSpec(memory_space=pltpu.SMEM)],
        out_specs=anywhere,
        scratch_shapes=[
            pltpu.VMEM((NH, ROWS, WIDTH), bf),
            pltpu.VMEM((NEARROWS, 2 * DH), bf),
            pltpu.VMEM((MIDK, 2 * DH), bf),
            pltpu.VMEM((NVB * VW, 2 * DH), bf),
            pltpu.VMEM((NVB * VW, 2 * DH), bf),
            pltpu.VMEM((3, QUART, 2 * DH), bf),
            pltpu.VMEM((QUART, 2 * DH), bf),
            pltpu.VMEM((4, ROWS, 2 * DH), bf),
            pltpu.VMEM((ROWS, 2 * DH), bf),
            pltpu.VMEM((NH, ROWS, WIDTH), bf),
            pltpu.VMEM((2, M, RESTK), jnp.float32),
            pltpu.VMEM((2, M, VW), jnp.float32),
            pltpu.VMEM((NH, M, 2 * DH), jnp.float32),
            pltpu.VMEM((NH, M, VW), jnp.float32),
            dma((8,)), dma((NH,)), dma((NH,)), dma((NH,)), dma((NH,)),
            dma((8,)), dma((4, NPIECE)), *[dma((4,)) for _ in range(8)], dma((NH,)), dma((NH,)),
            pltpu.SemaphoreType.REGULAR((4,)), pltpu.SemaphoreType.REGULAR((4,)),
        ],
        compiler_params=pltpu.CompilerParams(
            collective_id=0, has_side_effects=True, vmem_limit_bytes=32 * 2**20),
        name="sparse_attention",
    )(queries, keys, values, vert_blocks)


def solution(mesh):
    placed = (
        P(("ctx", "head"), None),
        P(("ctx", "head"), None),
        P(("ctx", "head"), None),
        P("head", None),
    )
    return jax.shard_map(
        per_device, mesh=mesh, in_specs=placed, out_specs=P(("ctx", "head"), None), check_vma=False
    )
```

```python
import functools
import math

import jax
import jax.numpy as jnp
from jax import lax
from jax.experimental import pallas as pl
from jax.experimental.pallas import tpu as pltpu
from jax.sharding import PartitionSpec as P

DH = 128
VW = 128
NVB = 8
NC = 16
NH = 8
ROWS = 64
SLAB = 512
BAND = 2048
HPG = 8
WIDTH = HPG * DH
M = ROWS * HPG
NEARK = SLAB + 2 * ROWS
NEARROWS = 2 * SLAB + ROWS
MIDK = 3 * SLAB
RESTK = MIDK + NVB * VW
KB = 256
PIECE = 128
NPIECE = SLAB // PIECE
QUART = 256
NEG = -1e30
SCALE = math.log2(math.e) / math.sqrt(float(DH))

def cut(kind, size, col):
    return [(kind, o, min(KB, size - o), col + o) for o in range(0, size, KB)]


NEAR = cut(0, NEARK, 0)
REST = cut(1, MIDK, 0) + cut(2, NVB * VW, MIDK)


def kernel(
    q_hbm, k_hbm, v_hbm, vb_ref, out_hbm,
    qb, near, mid, vt, tb, rb, ub, zb, ch, ob, s_ref, m_ref, va, vm,
    loc, kvs, kvr, qs, qr, bs, br,
    sxs, sxr, szs, szr, gzs, gzr, gxs, gxr, os_, or_, rx, rz,
):
    c = lax.axis_index("ctx")
    h = lax.axis_index("head")
    x = c // 4
    z = c % 4
    y = h // 2
    core = h % 2

    def remote(src, dst, ssem, rsem, cc, hh):
        return pltpu.make_async_remote_copy(
            src_ref=src, dst_ref=dst, send_sem=ssem, recv_sem=rsem,
            device_id={"ctx": cc, "head": hh}, device_id_type=pl.DeviceIdType.MESH,
        )

    def drain(ref, sem):
        pltpu.make_async_copy(ref, ref, sem).wait()

    def offset(i):
        r = i % 3
        dy = jnp.where(i < 6, 2 - r + 3 * (r // 2), 0)
        dc = jnp.where(i < 6, i // 3, 7 - i)
        return dy, dc

    def source(i):
        dy, dc = offset(i)
        return ((y + dy) % 4) * 2 + (core + dc) % 2

    def target(i):
        dy, dc = offset(i)
        return ((y + 4 - dy) % 4) * 2 + (core + 2 - dc) % 2

    def pick(shape, b):
        return jnp.zeros(shape, jnp.int32) + vb_ref[0, b]

    def choose(cases):
        r = jnp.zeros(cases[0][1].shape, jnp.float32)
        for mask, value in cases:
            r = jnp.where(mask, value.astype(jnp.float32), r)
        return r.astype(jnp.bfloat16)

    mine = pl.ds(pl.multiple_of(SLAB + h * ROWS, ROWS), ROWS)
    own_k = pltpu.make_async_copy(
        k_hbm.at[:, pl.ds(pl.multiple_of(h * DH, DH), DH)], near.at[mine, pl.ds(0, DH)], loc.at[0])
    own_v = pltpu.make_async_copy(
        v_hbm.at[:, pl.ds(pl.multiple_of(h * DH, DH), DH)], near.at[mine, pl.ds(DH, DH)], loc.at[1])
    own_q = pltpu.make_async_copy(
        q_hbm.at[:, pl.ds(pl.multiple_of(h * WIDTH, WIDTH), WIDTH)], qb.at[h], loc.at[2])
    own_k.start()
    own_v.start()
    own_q.start()

    barrier = pltpu.get_barrier_semaphore()

    def at(xx, zz):
        return xx * 4 + zz

    def signal(sem, cc, hh):
        pl.semaphore_signal(sem, inc=1, device_id={"ctx": cc, "head": hh},
                            device_id_type=pl.DeviceIdType.MESH)

    for d in range(1, NH):
        signal(barrier, c, (h + d) % NH)
    for n in range(1, 4):
        @pl.when(n > x)
        def _():
            signal(barrier, at(n, z), h)

        @pl.when(n > z)
        def _():
            signal(barrier, at(x, n), h)
    near[pl.ds(2 * SLAB, ROWS), :] = jnp.zeros((ROWS, 2 * DH), jnp.bfloat16)

    @pl.when(c < 4)
    def _():
        near[pl.ds(0, SLAB), :] = jnp.zeros((SLAB, 2 * DH), jnp.bfloat16)
        vt[...] = jnp.zeros_like(vt)
        for d in range(1, 4):
            @pl.when(c < d)
            def _():
                mid[pl.ds((3 - d) * SLAB, SLAB), :] = jnp.zeros((SLAB, 2 * DH), jnp.bfloat16)

    pl.semaphore_wait(barrier, NH - 1 + x + z)
    for n in range(3):
        @pl.when(n < x)
        def _():
            signal(rx.at[x], at(n, z), h)

        @pl.when(n < z)
        def _():
            signal(rz.at[z], at(x, n), h)

    def kv_copies(i):
        t = target(i)
        return [
            remote(src.at[:, pl.ds(pl.multiple_of(t * DH, DH), DH)],
                   near.at[mine, pl.ds(n * DH, DH)], kvs.at[t], kvr.at[h], c, t)
            for n, src in enumerate((k_hbm, v_hbm))
        ]

    def q_copy(i):
        t = target(i)
        return remote(q_hbm.at[:, pl.ds(pl.multiple_of(t * WIDTH, WIDTH), WIDTH)],
                      qb.at[h], qs.at[t], qr.at[h], c, t)

    for i in range(7):
        for cp in kv_copies(i):
            cp.start()
    q_copy(6).start()

    for i in range(6):
        q_copy(i).start()
    own_k.wait()
    own_v.wait()
    for i in range(7):
        s = source(i)
        drain(near.at[pl.ds(pl.multiple_of(SLAB + s * ROWS, ROWS), ROWS), :], kvr.at[s])
    for n in range(1, 4):
        @pl.when(n > x)
        def _():
            pl.semaphore_wait(rx.at[n], 1)

        @pl.when(n > z)
        def _():
            pl.semaphore_wait(rz.at[n], 1)

    def part(d, start, rows):
        if d == 0 or d == 4:
            return near.at[pl.ds(start + (SLAB if d == 0 else 0), rows), :]
        return mid.at[pl.ds(start + (3 - d) * SLAB, rows), :]

    def slab(d):
        return part(d, 0, SLAB)

    def piece(d, k):
        return part(d, k * PIECE, PIECE)

    def hop(n, cond, d_src, d_dst, cc, k):
        @pl.when(cond)
        def _():
            remote(piece(d_src, k), piece(d_dst, k), bs.at[n], br.at[d_dst - 1, k], cc, h).start()

    def landed(d, k):
        @pl.when(c >= d)
        def _():
            drain(piece(d, k), br.at[d - 1, k])

    middle = (z == 1) | (z == 2)
    back = x > 0

    quarter = pl.ds(pl.multiple_of(x * QUART, QUART), QUART)
    chunk = pl.ds(pl.multiple_of(x * QUART + z * ROWS, ROWS), ROWS)

    def local(src, dst, sem):
        cp = pltpu.make_async_copy(src, dst, sem)
        cp.start()
        return cp

    def total(parts):
        r = parts[0].astype(jnp.float32)
        for e in parts[1:]:
            r = r + e.astype(jnp.float32)
        return r.astype(jnp.bfloat16)

    def table_add_x():
        @pl.when(x < 3)
        def _():
            for b in range(NVB):
                place = pick((VW, 2 * DH), b) - 4 * c
                tb[pl.ds(b * VW, VW), :] = choose(
                    [(place == n, near[pl.ds(SLAB + n * VW, VW), :]) for n in range(4)])
            for n in range(4):
                @pl.when(n != x)
                def _():
                    remote(tb.at[pl.ds(n * QUART, QUART), :], rb.at[x],
                           sxs.at[n], sxr.at[x], at(n, z), h).start()
            local(tb.at[quarter, :], rb.at[x], loc.at[3]).wait()

    def table_add_z():
        for n in range(3):
            @pl.when(n != x)
            def _():
                drain(rb.at[n], sxr.at[n])
        ub[...] = total([rb[n] for n in range(3)])
        for n in range(4):
            @pl.when(n != z)
            def _():
                remote(ub.at[pl.ds(n * ROWS, ROWS), :], zb.at[z],
                       szs.at[n], szr.at[z], at(x, n), h).start()
        local(ub.at[pl.ds(pl.multiple_of(z * ROWS, ROWS), ROWS), :], zb.at[z], loc.at[3]).wait()

    def table_gather_z():
        for n in range(4):
            @pl.when(n != z)
            def _():
                drain(zb.at[n], szr.at[n])
        ch[...] = total([zb[n] for n in range(4)])
        for n in range(4):
            @pl.when(n != z)
            def _():
                remote(ch, vt.at[chunk, :], gzs.at[n], gzr.at[z], at(x, n), h).start()
        table_across(ch, chunk)
        local(ch, vt.at[chunk, :], loc.at[4]).wait()

    def table_across(src, rows):
        for n in range(1, 4):
            @pl.when(n != x)
            def _():
                remote(src, vt.at[rows, :], gxs.at[n], gxr.at[x], at(n, z), h).start()

    def table_gather_x():
        for n in range(4):
            @pl.when(n != z)
            def _():
                drain(ch, gzr.at[n])
                rows = pl.ds(pl.multiple_of(x * QUART + n * ROWS, ROWS), ROWS)
                table_across(vt.at[rows, :], rows)

    def table_wait():
        for n in range(4):
            @pl.when((x > 0) & (n != x))
            def _():
                drain(vt.at[pl.ds(n * QUART, QUART), :], gxr.at[n])

    table_add_x()
    for k in range(NPIECE):
        hop(2, x < 3, 0, 4, c + 4, k)
    for k in range(NPIECE):
        hop(0, z < 3, 0, 1, c + 1, k)
        hop(1, z == 0, 0, 3, c + 3, k)
    table_add_z()
    for k in range(NPIECE):
        landed(4, k)
        hop(3, back & (z > 0), 4, 3, c - 1, k)
        hop(4, back & (z == 3), 4, 1, c - 3, k)
    table_gather_z()
    for k in range(NPIECE):
        landed(1, k)
        hop(5, middle, 1, 2, c + 1, k)
    table_gather_x()
    for k in range(NPIECE):
        landed(3, k)
        hop(6, back & middle, 3, 2, c - 1, k)

    ii = lax.broadcasted_iota(jnp.int32, (ROWS, VW), 0)
    jj = lax.broadcasted_iota(jnp.int32, (ROWS, VW), 1)
    missing = (jnp.where(c < 4, SLAB, 0), jnp.maximum(3 - c, 0) * SLAB)

    def keep(mask, t):
        return jnp.where(mask[None], t.reshape(HPG, ROWS, VW), NEG).reshape(M, VW)

    def load_q(p):
        return jnp.concatenate([qb[p, :, n * DH:(n + 1) * DH] for n in range(HPG)], axis=0)

    def load(p, blk, column):
        kind, off, w, _ = blk
        cols = pl.ds(column * DH, DH)
        if kind == 0:
            return near[pl.ds(pl.multiple_of(p * ROWS, ROWS) + off, w), cols]
        return mid[pl.ds(off, w), cols] if kind == 1 else vt[pl.ds(off, w), cols]

    def scores(p, q, blk, slot, mx):
        kind, off, w, col = blk
        k = load(p, blk, 0)
        s = lax.dot_general(q, k, (((1,), (1,)), ((), ())), preferred_element_type=jnp.float32)
        for t in range(w // VW):
            e = s[:, t * VW:(t + 1) * VW]
            o = off + t * VW
            if kind == 0:
                mask = jj >= missing[0] - p * ROWS - o
                if o == 0:
                    mask = mask & (jj > ii)
                if o + VW == NEARK:
                    mask = mask & (jj <= ii)
            elif kind == 1:
                mask = jj >= missing[1] - o
            else:
                mask = (jj - ii + pick((ROWS, VW), o // VW) * VW) <= (c * SLAB + p * ROWS - BAND)
            e = keep(mask, e)
            mx = e if mx is None else jnp.maximum(mx, e)
            s_ref[slot, :, col + t * VW:col + (t + 1) * VW] = e
        return mx

    def row_max(mx):
        return jnp.broadcast_to(jnp.max(mx, axis=1, keepdims=True) * SCALE, (M, VW))

    def weigh(p, blk, slot, acc):
        kind, off, w, col = blk
        v = load(p, blk, 1)
        v = jnp.concatenate([v, jnp.ones((w, DH), jnp.bfloat16)], axis=1)
        m = m_ref[slot]
        e = [jnp.exp2(s_ref[slot, :, col + t * VW:col + (t + 1) * VW] * SCALE - m).astype(jnp.bfloat16)
             for t in range(w // VW)]
        d = jnp.dot(jnp.concatenate(e, axis=1), v, preferred_element_type=jnp.float32)
        return d if acc is None else acc + d

    def out_copy(p):
        return remote(ob.at[p], out_hbm.at[:, pl.ds(pl.multiple_of(h * WIDTH, WIDTH), WIDTH)],
                      os_.at[p], or_.at[h], c, p)

    def unit_loop(blocks, before, top, after):
        def begin(i):
            before(i)
            return source(i)

        def stage(i, slot):
            p = source(i)
            n = begin(jnp.minimum(i + 1, 7))
            q = load_q(n)
            acc = mx = None
            for blk in blocks:
                mx = scores(n, q, blk, 1 - slot, mx)
                acc = weigh(p, blk, slot, acc)
            after(i, p, slot, acc)
            m_ref[1 - slot] = top(n, row_max(mx))

        n = begin(0)
        q = load_q(n)
        mx = None
        for blk in blocks:
            mx = scores(n, q, blk, 0, mx)
        m_ref[0] = top(n, row_max(mx))

        def body(t, carry):
            stage(2 * t, 0)
            stage(2 * t + 1, 1)
            return carry

        lax.fori_loop(0, 4, body, 0)

    own_q.wait()

    def q_arrived(i):
        @pl.when(i < 7)
        def _():
            n = source(i)
            drain(qb.at[n], qr.at[n])

    def keep_near(i, p, slot, acc):
        va[p] = acc
        vm[p] = m_ref[slot]

    unit_loop(NEAR, q_arrived, lambda n, m: m, keep_near)

    for k in range(NPIECE):
        landed(2, k)
    table_wait()

    def finish(i, p, slot, acc):
        f = jnp.exp2(vm[p] - m_ref[slot])
        acc = acc + va[p] * jnp.concatenate([f, f], axis=1)
        o = (acc[:, :DH] / acc[:, DH:]).astype(jnp.bfloat16)
        for t in range(HPG):
            ob[p, :, t * DH:(t + 1) * DH] = o[t * ROWS:(t + 1) * ROWS]

        @pl.when(i < 7)
        def _():
            out_copy(p).start()

    unit_loop(REST, lambda i: None, lambda n, m: jnp.maximum(m, vm[n]), finish)

    own_o = pltpu.make_async_copy(
        ob.at[h], out_hbm.at[:, pl.ds(pl.multiple_of(h * WIDTH, WIDTH), WIDTH)], loc.at[5])
    own_o.start()

    for i in range(7):
        t = target(i)
        for cp in kv_copies(i):
            cp.wait_send()
        q_copy(i).wait_send()
    for n, cond, d in (
        (0, z < 3, 0), (1, z == 0, 0), (2, x < 3, 0), (3, back & (z > 0), 4),
        (4, back & (z == 3), 4), (5, middle, 1), (6, back & middle, 3),
    ):
        @pl.when(cond)
        def _():
            drain(slab(d), bs.at[n])

    for n in range(4):
        @pl.when((x < 3) & (n != x))
        def _():
            drain(rb.at[0], sxs.at[n])

        @pl.when(n != z)
        def _():
            drain(ch, szs.at[n])
            drain(ch, gzs.at[n])

        if n > 0:
            @pl.when(n != x)
            def _():
                drain(rb.at[0], gxs.at[n])
    for i in range(7):
        p = source(i)
        drain(ob.at[p], os_.at[p])
        drain(out_hbm.at[:, pl.ds(pl.multiple_of(p * WIDTH, WIDTH), WIDTH)], or_.at[p])
    own_o.wait()


def per_device(queries, keys, values, vert_blocks):
    anywhere = pl.BlockSpec(memory_space=pl.ANY)
    queries, keys, values, vert_blocks = (
        pltpu.with_memory_space_constraint(e, pltpu.HBM)
        for e in (queries, keys, values, vert_blocks))
    dma = pltpu.SemaphoreType.DMA
    bf = jnp.bfloat16
    return pl.pallas_call(
        kernel,
        out_shape=jax.ShapeDtypeStruct((ROWS, NH * WIDTH), bf),
        in_specs=[anywhere, anywhere, anywhere, pl.BlockSpec(memory_space=pltpu.SMEM)],
        out_specs=anywhere,
        scratch_shapes=[
            pltpu.VMEM((NH, ROWS, WIDTH), bf),
            pltpu.VMEM((NEARROWS, 2 * DH), bf),
            pltpu.VMEM((MIDK, 2 * DH), bf),
            pltpu.VMEM((NVB * VW, 2 * DH), bf),
            pltpu.VMEM((NVB * VW, 2 * DH), bf),
            pltpu.VMEM((3, QUART, 2 * DH), bf),
            pltpu.VMEM((QUART, 2 * DH), bf),
            pltpu.VMEM((4, ROWS, 2 * DH), bf),
            pltpu.VMEM((ROWS, 2 * DH), bf),
            pltpu.VMEM((NH, ROWS, WIDTH), bf),
            pltpu.VMEM((2, M, RESTK), jnp.float32),
            pltpu.VMEM((2, M, VW), jnp.float32),
            pltpu.VMEM((NH, M, 2 * DH), jnp.float32),
            pltpu.VMEM((NH, M, VW), jnp.float32),
            dma((8,)), dma((NH,)), dma((NH,)), dma((NH,)), dma((NH,)),
            dma((8,)), dma((4, NPIECE)), *[dma((4,)) for _ in range(8)], dma((NH,)), dma((NH,)),
            pltpu.SemaphoreType.REGULAR((4,)), pltpu.SemaphoreType.REGULAR((4,)),
        ],
        compiler_params=pltpu.CompilerParams(
            collective_id=0, has_side_effects=True, vmem_limit_bytes=32 * 2**20),
        name="sparse_attention",
    )(queries, keys, values, vert_blocks)


def solution(mesh):
    placed = (
        P(("ctx", "head"), None),
        P(("ctx", "head"), None),
        P(("ctx", "head"), None),
        P("head", None),
    )
    return jax.shard_map(
        per_device, mesh=mesh, in_specs=placed, out_specs=P(("ctx", "head"), None), check_vma=False
    )
```

```python
import functools
import math

import jax
import jax.numpy as jnp
from jax import lax
from jax.experimental import pallas as pl
from jax.experimental.pallas import tpu as pltpu
from jax.sharding import PartitionSpec as P

DH = 128
VW = 128
NVB = 8
NC = 16
NH = 8
ROWS = 64
SLAB = 512
BAND = 2048
HPG = 8
WIDTH = HPG * DH
M = ROWS * HPG
NEARK = SLAB + 2 * ROWS
NEARROWS = 2 * SLAB + ROWS
MIDK = 3 * SLAB
RESTK = MIDK + NVB * VW
KB = 256
PIECE = 128
NPIECE = SLAB // PIECE
QUART = 256
NEG = -1e30
SCALE = math.log2(math.e) / math.sqrt(float(DH))

def cut(kind, size, col):
    return [(kind, o, min(KB, size - o), col + o) for o in range(0, size, KB)]


NEAR = cut(0, NEARK, 0)
REST = cut(1, MIDK, 0) + cut(2, NVB * VW, MIDK)


def kernel(
    q_hbm, k_hbm, v_hbm, vb_ref, out_hbm,
    qb, near, mid, vt, tb, rb, ub, zb, ch, ob, s_ref, m_ref, va, vm,
    loc, kvs, kvr, qs, qr, bs, br,
    sxs, sxr, szs, szr, gzs, gzr, gxs, gxr, os_, or_, rx, rz,
):
    c = lax.axis_index("ctx")
    h = lax.axis_index("head")
    x = c // 4
    z = c % 4
    y = h // 2
    core = h % 2

    def remote(src, dst, ssem, rsem, cc, hh):
        return pltpu.make_async_remote_copy(
            src_ref=src, dst_ref=dst, send_sem=ssem, recv_sem=rsem,
            device_id={"ctx": cc, "head": hh}, device_id_type=pl.DeviceIdType.MESH,
        )

    def drain(ref, sem):
        pltpu.make_async_copy(ref, ref, sem).wait()

    def offset(i):
        r = i % 3
        dy = jnp.where(i < 6, 2 - r + 3 * (r // 2), 0)
        dc = jnp.where(i < 6, i // 3, 7 - i)
        return dy, dc

    def source(i):
        dy, dc = offset(i)
        return ((y + dy) % 4) * 2 + (core + dc) % 2

    def target(i):
        dy, dc = offset(i)
        return ((y + 4 - dy) % 4) * 2 + (core + 2 - dc) % 2

    def pick(shape, b):
        return jnp.zeros(shape, jnp.int32) + vb_ref[0, b]

    def choose(cases):
        r = jnp.zeros(cases[0][1].shape, jnp.float32)
        for mask, value in cases:
            r = jnp.where(mask, value.astype(jnp.float32), r)
        return r.astype(jnp.bfloat16)

    mine = pl.ds(pl.multiple_of(SLAB + h * ROWS, ROWS), ROWS)
    own_k = pltpu.make_async_copy(
        k_hbm.at[:, pl.ds(pl.multiple_of(h * DH, DH), DH)], near.at[mine, pl.ds(0, DH)], loc.at[0])
    own_v = pltpu.make_async_copy(
        v_hbm.at[:, pl.ds(pl.multiple_of(h * DH, DH), DH)], near.at[mine, pl.ds(DH, DH)], loc.at[1])
    own_q = pltpu.make_async_copy(
        q_hbm.at[:, pl.ds(pl.multiple_of(h * WIDTH, WIDTH), WIDTH)], qb.at[h], loc.at[2])
    own_k.start()
    own_v.start()
    own_q.start()

    barrier = pltpu.get_barrier_semaphore()

    def at(xx, zz):
        return xx * 4 + zz

    def signal(sem, cc, hh):
        pl.semaphore_signal(sem, inc=1, device_id={"ctx": cc, "head": hh},
                            device_id_type=pl.DeviceIdType.MESH)

    for d in range(1, NH):
        signal(barrier, c, (h + d) % NH)
    for n in range(1, 4):
        @pl.when(n > x)
        def _():
            signal(barrier, at(n, z), h)

        @pl.when(n > z)
        def _():
            signal(barrier, at(x, n), h)
    near[pl.ds(2 * SLAB, ROWS), :] = jnp.zeros((ROWS, 2 * DH), jnp.bfloat16)

    @pl.when(c < 4)
    def _():
        near[pl.ds(0, SLAB), :] = jnp.zeros((SLAB, 2 * DH), jnp.bfloat16)
        vt[...] = jnp.zeros_like(vt)
        for d in range(1, 4):
            @pl.when(c < d)
            def _():
                mid[pl.ds((3 - d) * SLAB, SLAB), :] = jnp.zeros((SLAB, 2 * DH), jnp.bfloat16)

    pl.semaphore_wait(barrier, NH - 1 + x + z)
    for n in range(3):
        @pl.when(n < x)
        def _():
            signal(rx.at[x], at(n, z), h)

        @pl.when(n < z)
        def _():
            signal(rz.at[z], at(x, n), h)

    def kv_copies(i):
        t = target(i)
        return [
            remote(src.at[:, pl.ds(pl.multiple_of(t * DH, DH), DH)],
                   near.at[mine, pl.ds(n * DH, DH)], kvs.at[t], kvr.at[h], c, t)
            for n, src in enumerate((k_hbm, v_hbm))
        ]

    def q_copy(i):
        t = target(i)
        return remote(q_hbm.at[:, pl.ds(pl.multiple_of(t * WIDTH, WIDTH), WIDTH)],
                      qb.at[h], qs.at[t], qr.at[h], c, t)

    for i in range(7):
        for cp in kv_copies(i):
            cp.start()
    q_copy(6).start()

    for i in range(6):
        q_copy(i).start()
    own_k.wait()
    own_v.wait()
    for i in range(7):
        s = source(i)
        drain(near.at[pl.ds(pl.multiple_of(SLAB + s * ROWS, ROWS), ROWS), :], kvr.at[s])
    for n in range(1, 4):
        @pl.when(n > x)
        def _():
            pl.semaphore_wait(rx.at[n], 1)

        @pl.when(n > z)
        def _():
            pl.semaphore_wait(rz.at[n], 1)

    def part(d, start, rows):
        if d == 0 or d == 4:
            return near.at[pl.ds(start + (SLAB if d == 0 else 0), rows), :]
        return mid.at[pl.ds(start + (3 - d) * SLAB, rows), :]

    def slab(d):
        return part(d, 0, SLAB)

    def piece(d, k):
        return part(d, k * PIECE, PIECE)

    def hop(n, cond, d_src, d_dst, cc, k):
        @pl.when(cond)
        def _():
            remote(piece(d_src, k), piece(d_dst, k), bs.at[n], br.at[d_dst - 1, k], cc, h).start()

    def landed(d, k):
        @pl.when(c >= d)
        def _():
            drain(piece(d, k), br.at[d - 1, k])

    middle = (z == 1) | (z == 2)
    back = x > 0

    quarter = pl.ds(pl.multiple_of(x * QUART, QUART), QUART)
    chunk = pl.ds(pl.multiple_of(x * QUART + z * ROWS, ROWS), ROWS)

    def local(src, dst, sem):
        cp = pltpu.make_async_copy(src, dst, sem)
        cp.start()
        return cp

    def total(parts):
        r = parts[0].astype(jnp.float32)
        for e in parts[1:]:
            r = r + e.astype(jnp.float32)
        return r.astype(jnp.bfloat16)

    def table_add_x():
        @pl.when(x < 3)
        def _():
            for b in range(NVB):
                place = pick((VW, 2 * DH), b) - 4 * c
                tb[pl.ds(b * VW, VW), :] = choose(
                    [(place == n, near[pl.ds(SLAB + n * VW, VW), :]) for n in range(4)])
            for n in range(4):
                @pl.when(n != x)
                def _():
                    remote(tb.at[pl.ds(n * QUART, QUART), :], rb.at[x],
                           sxs.at[n], sxr.at[x], at(n, z), h).start()
            local(tb.at[quarter, :], rb.at[x], loc.at[3]).wait()

    def table_add_z():
        for n in range(3):
            @pl.when(n != x)
            def _():
                drain(rb.at[n], sxr.at[n])
        ub[...] = total([rb[n] for n in range(3)])
        for n in range(4):
            @pl.when(n != z)
            def _():
                remote(ub.at[pl.ds(n * ROWS, ROWS), :], zb.at[z],
                       szs.at[n], szr.at[z], at(x, n), h).start()
        local(ub.at[pl.ds(pl.multiple_of(z * ROWS, ROWS), ROWS), :], zb.at[z], loc.at[3]).wait()

    def table_gather_z():
        for n in range(4):
            @pl.when(n != z)
            def _():
                drain(zb.at[n], szr.at[n])
        ch[...] = total([zb[n] for n in range(4)])
        for n in range(4):
            @pl.when(n != z)
            def _():
                remote(ch, vt.at[chunk, :], gzs.at[n], gzr.at[z], at(x, n), h).start()
        table_across(ch, chunk)
        local(ch, vt.at[chunk, :], loc.at[4]).wait()

    def table_across(src, rows):
        for n in range(1, 4):
            @pl.when(n != x)
            def _():
                remote(src, vt.at[rows, :], gxs.at[n], gxr.at[x], at(n, z), h).start()

    def table_gather_x():
        for n in range(4):
            @pl.when(n != z)
            def _():
                drain(ch, gzr.at[n])
                rows = pl.ds(pl.multiple_of(x * QUART + n * ROWS, ROWS), ROWS)
                table_across(vt.at[rows, :], rows)

    def table_wait():
        for n in range(4):
            @pl.when((x > 0) & (n != x))
            def _():
                drain(vt.at[pl.ds(n * QUART, QUART), :], gxr.at[n])

    table_add_x()
    for k in range(NPIECE):
        hop(2, x < 3, 0, 4, c + 4, k)
    for k in range(NPIECE):
        hop(0, z < 3, 0, 1, c + 1, k)
        hop(1, z == 0, 0, 3, c + 3, k)
    table_add_z()
    for k in range(NPIECE):
        landed(4, k)
        hop(3, back & (z > 0), 4, 3, c - 1, k)
        hop(4, back & (z == 3), 4, 1, c - 3, k)
    table_gather_z()
    for k in range(NPIECE):
        landed(1, k)
        hop(5, middle, 1, 2, c + 1, k)
    table_gather_x()
    for k in range(NPIECE):
        landed(3, k)
        hop(6, back & middle, 3, 2, c - 1, k)

    ii = lax.broadcasted_iota(jnp.int32, (ROWS, VW), 0)
    jj = lax.broadcasted_iota(jnp.int32, (ROWS, VW), 1)
    missing = (jnp.where(c < 4, SLAB, 0), jnp.maximum(3 - c, 0) * SLAB)

    def keep(mask, t):
        return jnp.where(mask[None], t.reshape(HPG, ROWS, VW), NEG).reshape(M, VW)

    def load_q(p):
        return jnp.concatenate([qb[p, :, n * DH:(n + 1) * DH] for n in range(HPG)], axis=0)

    def load(p, blk, column):
        kind, off, w, _ = blk
        cols = pl.ds(column * DH, DH)
        if kind == 0:
            return near[pl.ds(pl.multiple_of(p * ROWS, ROWS) + off, w), cols]
        return mid[pl.ds(off, w), cols] if kind == 1 else vt[pl.ds(off, w), cols]

    def scores(p, q, blk, slot, mx):
        kind, off, w, col = blk
        k = load(p, blk, 0)
        s = lax.dot_general(q, k, (((1,), (1,)), ((), ())), preferred_element_type=jnp.float32)
        for t in range(w // VW):
            e = s[:, t * VW:(t + 1) * VW]
            o = off + t * VW
            if kind == 0:
                mask = jj >= missing[0] - p * ROWS - o
                if o == 0:
                    mask = mask & (jj > ii)
                if o + VW == NEARK:
                    mask = mask & (jj <= ii)
            elif kind == 1:
                mask = jj >= missing[1] - o
            else:
                mask = (jj - ii + pick((ROWS, VW), o // VW) * VW) <= (c * SLAB + p * ROWS - BAND)
            e = keep(mask, e)
            mx = e if mx is None else jnp.maximum(mx, e)
            s_ref[slot, :, col + t * VW:col + (t + 1) * VW] = e
        return mx

    def row_max(mx):
        return jnp.broadcast_to(jnp.max(mx, axis=1, keepdims=True) * SCALE, (M, VW))

    def weigh(p, blk, slot, acc):
        kind, off, w, col = blk
        v = load(p, blk, 1)
        v = jnp.concatenate([v, jnp.ones((w, DH), jnp.bfloat16)], axis=1)
        m = m_ref[slot]
        e = [jnp.exp2(s_ref[slot, :, col + t * VW:col + (t + 1) * VW] * SCALE - m).astype(jnp.bfloat16)
             for t in range(w // VW)]
        d = jnp.dot(jnp.concatenate(e, axis=1), v, preferred_element_type=jnp.float32)
        return d if acc is None else acc + d

    def out_copy(p):
        return remote(ob.at[p], out_hbm.at[:, pl.ds(pl.multiple_of(h * WIDTH, WIDTH), WIDTH)],
                      os_.at[p], or_.at[h], c, p)

    def unit_loop(blocks, before, top, after):
        def begin(i):
            before(i)
            return source(i)

        def stage(i, slot):
            p = source(i)
            n = begin(jnp.minimum(i + 1, 7))
            q = load_q(n)
            acc = mx = None
            for blk in blocks:
                mx = scores(n, q, blk, 1 - slot, mx)
                acc = weigh(p, blk, slot, acc)
            after(i, p, slot, acc)
            m_ref[1 - slot] = top(n, row_max(mx))

        n = begin(0)
        q = load_q(n)
        mx = None
        for blk in blocks:
            if blk[0] == 2 and blk[1] == 0:
                table_wait()
            mx = scores(n, q, blk, 0, mx)
        m_ref[0] = top(n, row_max(mx))

        def body(t, carry):
            stage(2 * t, 0)
            stage(2 * t + 1, 1)
            return carry

        lax.fori_loop(0, 4, body, 0)

    own_q.wait()

    def q_arrived(i):
        @pl.when(i < 7)
        def _():
            n = source(i)
            drain(qb.at[n], qr.at[n])

    def keep_near(i, p, slot, acc):
        va[p] = acc
        vm[p] = m_ref[slot]

    unit_loop(NEAR, q_arrived, lambda n, m: m, keep_near)

    for k in range(NPIECE):
        landed(2, k)

    def finish(i, p, slot, acc):
        f = jnp.exp2(vm[p] - m_ref[slot])
        acc = acc + va[p] * jnp.concatenate([f, f], axis=1)
        o = (acc[:, :DH] / acc[:, DH:]).astype(jnp.bfloat16)
        for t in range(HPG):
            ob[p, :, t * DH:(t + 1) * DH] = o[t * ROWS:(t + 1) * ROWS]

        @pl.when(i < 7)
        def _():
            out_copy(p).start()

    unit_loop(REST, lambda i: None, lambda n, m: jnp.maximum(m, vm[n]), finish)

    own_o = pltpu.make_async_copy(
        ob.at[h], out_hbm.at[:, pl.ds(pl.multiple_of(h * WIDTH, WIDTH), WIDTH)], loc.at[5])
    own_o.start()

    for i in range(7):
        t = target(i)
        for cp in kv_copies(i):
            cp.wait_send()
        q_copy(i).wait_send()
    for n, cond, d in (
        (0, z < 3, 0), (1, z == 0, 0), (2, x < 3, 0), (3, back & (z > 0), 4),
        (4, back & (z == 3), 4), (5, middle, 1), (6, back & middle, 3),
    ):
        @pl.when(cond)
        def _():
            drain(slab(d), bs.at[n])

    for n in range(4):
        @pl.when((x < 3) & (n != x))
        def _():
            drain(rb.at[0], sxs.at[n])

        @pl.when(n != z)
        def _():
            drain(ch, szs.at[n])
            drain(ch, gzs.at[n])

        if n > 0:
            @pl.when(n != x)
            def _():
                drain(rb.at[0], gxs.at[n])
    for i in range(7):
        p = source(i)
        drain(ob.at[p], os_.at[p])
        drain(out_hbm.at[:, pl.ds(pl.multiple_of(p * WIDTH, WIDTH), WIDTH)], or_.at[p])
    own_o.wait()


def per_device(queries, keys, values, vert_blocks):
    anywhere = pl.BlockSpec(memory_space=pl.ANY)
    queries, keys, values, vert_blocks = (
        pltpu.with_memory_space_constraint(e, pltpu.HBM)
        for e in (queries, keys, values, vert_blocks))
    dma = pltpu.SemaphoreType.DMA
    bf = jnp.bfloat16
    return pl.pallas_call(
        kernel,
        out_shape=jax.ShapeDtypeStruct((ROWS, NH * WIDTH), bf),
        in_specs=[anywhere, anywhere, anywhere, pl.BlockSpec(memory_space=pltpu.SMEM)],
        out_specs=anywhere,
        scratch_shapes=[
            pltpu.VMEM((NH, ROWS, WIDTH), bf),
            pltpu.VMEM((NEARROWS, 2 * DH), bf),
            pltpu.VMEM((MIDK, 2 * DH), bf),
            pltpu.VMEM((NVB * VW, 2 * DH), bf),
            pltpu.VMEM((NVB * VW, 2 * DH), bf),
            pltpu.VMEM((3, QUART, 2 * DH), bf),
            pltpu.VMEM((QUART, 2 * DH), bf),
            pltpu.VMEM((4, ROWS, 2 * DH), bf),
            pltpu.VMEM((ROWS, 2 * DH), bf),
            pltpu.VMEM((NH, ROWS, WIDTH), bf),
            pltpu.VMEM((2, M, RESTK), jnp.float32),
            pltpu.VMEM((2, M, VW), jnp.float32),
            pltpu.VMEM((NH, M, 2 * DH), jnp.float32),
            pltpu.VMEM((NH, M, VW), jnp.float32),
            dma((8,)), dma((NH,)), dma((NH,)), dma((NH,)), dma((NH,)),
            dma((8,)), dma((4, NPIECE)), *[dma((4,)) for _ in range(8)], dma((NH,)), dma((NH,)),
            pltpu.SemaphoreType.REGULAR((4,)), pltpu.SemaphoreType.REGULAR((4,)),
        ],
        compiler_params=pltpu.CompilerParams(
            collective_id=0, has_side_effects=True, vmem_limit_bytes=32 * 2**20),
        name="sparse_attention",
    )(queries, keys, values, vert_blocks)


def solution(mesh):
    placed = (
        P(("ctx", "head"), None),
        P(("ctx", "head"), None),
        P(("ctx", "head"), None),
        P("head", None),
    )
    return jax.shard_map(
        per_device, mesh=mesh, in_specs=placed, out_specs=P(("ctx", "head"), None), check_vma=False
    )
```

```python
import functools
import math

import jax
import jax.numpy as jnp
from jax import lax
from jax.experimental import pallas as pl
from jax.experimental.pallas import tpu as pltpu
from jax.sharding import PartitionSpec as P

DH = 128
VW = 128
NVB = 8
NC = 16
NH = 8
ROWS = 64
SLAB = 512
BAND = 2048
HPG = 8
WIDTH = HPG * DH
M = ROWS * HPG
NEARK = SLAB + 2 * ROWS
NEARROWS = 2 * SLAB + ROWS
MIDK = 3 * SLAB
RESTK = MIDK + NVB * VW
KB = 256
PIECE = 128
NPIECE = SLAB // PIECE
QUART = 256
NEG = -1e30
SCALE = math.log2(math.e) / math.sqrt(float(DH))

def cut(kind, size, col):
    return [(kind, o, min(KB, size - o), col + o) for o in range(0, size, KB)]


NEAR = cut(0, NEARK, 0)
REST = cut(1, MIDK, 0) + cut(2, NVB * VW, MIDK)


def kernel(
    q_hbm, k_hbm, v_hbm, vb_ref, out_hbm,
    qb, near, mid, vt, tb, rb, ub, zb, ch, ob, s_ref, m_ref, va, vm,
    loc, kvs, kvr, qs, qr, bs, br,
    sxs, sxr, szs, szr, gzs, gzr, gxs, gxr, os_, or_, rx, rz,
):
    c = lax.axis_index("ctx")
    h = lax.axis_index("head")
    x = c // 4
    z = c % 4
    y = h // 2
    core = h % 2

    def remote(src, dst, ssem, rsem, cc, hh):
        return pltpu.make_async_remote_copy(
            src_ref=src, dst_ref=dst, send_sem=ssem, recv_sem=rsem,
            device_id={"ctx": cc, "head": hh}, device_id_type=pl.DeviceIdType.MESH,
        )

    def drain(ref, sem):
        pltpu.make_async_copy(ref, ref, sem).wait()

    def offset(i):
        r = i % 3
        dy = jnp.where(i < 6, 2 - r + 3 * (r // 2), 0)
        dc = jnp.where(i < 6, i // 3, 7 - i)
        return dy, dc

    def source(i):
        dy, dc = offset(i)
        return ((y + dy) % 4) * 2 + (core + dc) % 2

    def target(i):
        dy, dc = offset(i)
        return ((y + 4 - dy) % 4) * 2 + (core + 2 - dc) % 2

    def pick(shape, b):
        return jnp.zeros(shape, jnp.int32) + vb_ref[0, b]

    def choose(cases):
        r = jnp.zeros(cases[0][1].shape, jnp.float32)
        for mask, value in cases:
            r = jnp.where(mask, value.astype(jnp.float32), r)
        return r.astype(jnp.bfloat16)

    mine = pl.ds(pl.multiple_of(SLAB + h * ROWS, ROWS), ROWS)
    own_k = pltpu.make_async_copy(
        k_hbm.at[:, pl.ds(pl.multiple_of(h * DH, DH), DH)], near.at[mine, pl.ds(0, DH)], loc.at[0])
    own_v = pltpu.make_async_copy(
        v_hbm.at[:, pl.ds(pl.multiple_of(h * DH, DH), DH)], near.at[mine, pl.ds(DH, DH)], loc.at[1])
    own_q = pltpu.make_async_copy(
        q_hbm.at[:, pl.ds(pl.multiple_of(h * WIDTH, WIDTH), WIDTH)], qb.at[h], loc.at[2])
    own_k.start()
    own_v.start()
    own_q.start()

    barrier = pltpu.get_barrier_semaphore()

    def at(xx, zz):
        return xx * 4 + zz

    def signal(sem, cc, hh):
        pl.semaphore_signal(sem, inc=1, device_id={"ctx": cc, "head": hh},
                            device_id_type=pl.DeviceIdType.MESH)

    for d in range(1, NH):
        signal(barrier, c, (h + d) % NH)
    for n in range(1, 4):
        @pl.when(n > x)
        def _():
            signal(barrier, at(n, z), h)

        @pl.when(n > z)
        def _():
            signal(barrier, at(x, n), h)
    near[pl.ds(2 * SLAB, ROWS), :] = jnp.zeros((ROWS, 2 * DH), jnp.bfloat16)

    @pl.when(c < 4)
    def _():
        near[pl.ds(0, SLAB), :] = jnp.zeros((SLAB, 2 * DH), jnp.bfloat16)
        vt[...] = jnp.zeros_like(vt)
        for d in range(1, 4):
            @pl.when(c < d)
            def _():
                mid[pl.ds((3 - d) * SLAB, SLAB), :] = jnp.zeros((SLAB, 2 * DH), jnp.bfloat16)

    pl.semaphore_wait(barrier, NH - 1 + x + z)
    for n in range(3):
        @pl.when(n < x)
        def _():
            signal(rx.at[x], at(n, z), h)

        @pl.when(n < z)
        def _():
            signal(rz.at[z], at(x, n), h)

    def kv_copies(i):
        t = target(i)
        return [
            remote(src.at[:, pl.ds(pl.multiple_of(t * DH, DH), DH)],
                   near.at[mine, pl.ds(n * DH, DH)], kvs.at[t], kvr.at[h], c, t)
            for n, src in enumerate((k_hbm, v_hbm))
        ]

    def q_copy(i):
        t = target(i)
        return remote(q_hbm.at[:, pl.ds(pl.multiple_of(t * WIDTH, WIDTH), WIDTH)],
                      qb.at[h], qs.at[t], qr.at[h], c, t)

    for i in range(7):
        for cp in kv_copies(i):
            cp.start()
    q_copy(6).start()

    for i in range(6):
        q_copy(i).start()
    own_k.wait()
    own_v.wait()
    for i in range(7):
        s = source(i)
        drain(near.at[pl.ds(pl.multiple_of(SLAB + s * ROWS, ROWS), ROWS), :], kvr.at[s])
    for n in range(1, 4):
        @pl.when(n > x)
        def _():
            pl.semaphore_wait(rx.at[n], 1)

        @pl.when(n > z)
        def _():
            pl.semaphore_wait(rz.at[n], 1)

    def part(d, start, rows):
        if d == 0 or d == 4:
            return near.at[pl.ds(start + (SLAB if d == 0 else 0), rows), :]
        return mid.at[pl.ds(start + (3 - d) * SLAB, rows), :]

    def slab(d):
        return part(d, 0, SLAB)

    def piece(d, k):
        return part(d, k * PIECE, PIECE)

    def hop(n, cond, d_src, d_dst, cc, k):
        @pl.when(cond)
        def _():
            remote(piece(d_src, k), piece(d_dst, k), bs.at[n], br.at[d_dst - 1, k], cc, h).start()

    def landed(d, k):
        @pl.when(c >= d)
        def _():
            drain(piece(d, k), br.at[d - 1, k])

    middle = (z == 1) | (z == 2)
    back = x > 0

    quarter = pl.ds(pl.multiple_of(x * QUART, QUART), QUART)
    chunk = pl.ds(pl.multiple_of(x * QUART + z * ROWS, ROWS), ROWS)

    def local(src, dst, sem):
        cp = pltpu.make_async_copy(src, dst, sem)
        cp.start()
        return cp

    def total(parts):
        r = parts[0].astype(jnp.float32)
        for e in parts[1:]:
            r = r + e.astype(jnp.float32)
        return r.astype(jnp.bfloat16)

    def table_add_x():
        @pl.when(x < 3)
        def _():
            for b in range(NVB):
                place = pick((VW, 2 * DH), b) - 4 * c
                tb[pl.ds(b * VW, VW), :] = choose(
                    [(place == n, near[pl.ds(SLAB + n * VW, VW), :]) for n in range(4)])
            for n in range(4):
                @pl.when(n != x)
                def _():
                    remote(tb.at[pl.ds(n * QUART, QUART), :], rb.at[x],
                           sxs.at[n], sxr.at[x], at(n, z), h).start()
            local(tb.at[quarter, :], rb.at[x], loc.at[3]).wait()

    def table_add_z():
        for n in range(3):
            @pl.when(n != x)
            def _():
                drain(rb.at[n], sxr.at[n])
        ub[...] = total([rb[n] for n in range(3)])
        for n in range(4):
            @pl.when(n != z)
            def _():
                remote(ub.at[pl.ds(n * ROWS, ROWS), :], zb.at[z],
                       szs.at[n], szr.at[z], at(x, n), h).start()
        local(ub.at[pl.ds(pl.multiple_of(z * ROWS, ROWS), ROWS), :], zb.at[z], loc.at[3]).wait()

    def table_gather_z():
        for n in range(4):
            @pl.when(n != z)
            def _():
                drain(zb.at[n], szr.at[n])
        ch[...] = total([zb[n] for n in range(4)])
        for n in range(4):
            @pl.when(n != z)
            def _():
                remote(ch, vt.at[chunk, :], gzs.at[n], gzr.at[z], at(x, n), h).start()
        table_across(ch, chunk)
        local(ch, vt.at[chunk, :], loc.at[4]).wait()

    def table_across(src, rows):
        for n in range(1, 4):
            @pl.when(n != x)
            def _():
                remote(src, vt.at[rows, :], gxs.at[n], gxr.at[x], at(n, z), h).start()

    def table_gather_x():
        for n in range(4):
            @pl.when(n != z)
            def _():
                drain(ch, gzr.at[n])
                rows = pl.ds(pl.multiple_of(x * QUART + n * ROWS, ROWS), ROWS)
                table_across(vt.at[rows, :], rows)

    def table_wait():
        for n in range(4):
            @pl.when((x > 0) & (n != x))
            def _():
                drain(vt.at[pl.ds(n * QUART, QUART), :], gxr.at[n])

    table_add_x()
    for k in range(NPIECE):
        hop(2, x < 3, 0, 4, c + 4, k)
    table_add_z()
    for k in range(NPIECE):
        hop(0, z < 3, 0, 1, c + 1, k)
        hop(1, z == 0, 0, 3, c + 3, k)
    for k in range(NPIECE):
        landed(4, k)
        hop(3, back & (z > 0), 4, 3, c - 1, k)
        hop(4, back & (z == 3), 4, 1, c - 3, k)
    table_gather_z()
    for k in range(NPIECE):
        landed(1, k)
        hop(5, middle, 1, 2, c + 1, k)
    table_gather_x()
    for k in range(NPIECE):
        landed(3, k)
        hop(6, back & middle, 3, 2, c - 1, k)

    ii = lax.broadcasted_iota(jnp.int32, (ROWS, VW), 0)
    jj = lax.broadcasted_iota(jnp.int32, (ROWS, VW), 1)
    missing = (jnp.where(c < 4, SLAB, 0), jnp.maximum(3 - c, 0) * SLAB)

    def keep(mask, t):
        return jnp.where(mask[None], t.reshape(HPG, ROWS, VW), NEG).reshape(M, VW)

    def load_q(p):
        return jnp.concatenate([qb[p, :, n * DH:(n + 1) * DH] for n in range(HPG)], axis=0)

    def load(p, blk, column):
        kind, off, w, _ = blk
        cols = pl.ds(column * DH, DH)
        if kind == 0:
            return near[pl.ds(pl.multiple_of(p * ROWS, ROWS) + off, w), cols]
        return mid[pl.ds(off, w), cols] if kind == 1 else vt[pl.ds(off, w), cols]

    def scores(p, q, blk, slot, mx):
        kind, off, w, col = blk
        k = load(p, blk, 0)
        s = lax.dot_general(q, k, (((1,), (1,)), ((), ())), preferred_element_type=jnp.float32)
        for t in range(w // VW):
            e = s[:, t * VW:(t + 1) * VW]
            o = off + t * VW
            if kind == 0:
                mask = jj >= missing[0] - p * ROWS - o
                if o == 0:
                    mask = mask & (jj > ii)
                if o + VW == NEARK:
                    mask = mask & (jj <= ii)
            elif kind == 1:
                mask = jj >= missing[1] - o
            else:
                mask = (jj - ii + pick((ROWS, VW), o // VW) * VW) <= (c * SLAB + p * ROWS - BAND)
            e = keep(mask, e)
            mx = e if mx is None else jnp.maximum(mx, e)
            s_ref[slot, :, col + t * VW:col + (t + 1) * VW] = e
        return mx

    def row_max(mx):
        return jnp.broadcast_to(jnp.max(mx, axis=1, keepdims=True) * SCALE, (M, VW))

    def weigh(p, blk, slot, acc):
        kind, off, w, col = blk
        v = load(p, blk, 1)
        v = jnp.concatenate([v, jnp.ones((w, DH), jnp.bfloat16)], axis=1)
        m = m_ref[slot]
        e = [jnp.exp2(s_ref[slot, :, col + t * VW:col + (t + 1) * VW] * SCALE - m).astype(jnp.bfloat16)
             for t in range(w // VW)]
        d = jnp.dot(jnp.concatenate(e, axis=1), v, preferred_element_type=jnp.float32)
        return d if acc is None else acc + d

    def out_copy(p):
        return remote(ob.at[p], out_hbm.at[:, pl.ds(pl.multiple_of(h * WIDTH, WIDTH), WIDTH)],
                      os_.at[p], or_.at[h], c, p)

    def unit_loop(blocks, before, top, after):
        def begin(i):
            before(i)
            return source(i)

        def stage(i, slot):
            p = source(i)
            n = begin(jnp.minimum(i + 1, 7))
            q = load_q(n)
            acc = mx = None
            for blk in blocks:
                mx = scores(n, q, blk, 1 - slot, mx)
                acc = weigh(p, blk, slot, acc)
            after(i, p, slot, acc)
            m_ref[1 - slot] = top(n, row_max(mx))

        n = begin(0)
        q = load_q(n)
        mx = None
        for blk in blocks:
            mx = scores(n, q, blk, 0, mx)
        m_ref[0] = top(n, row_max(mx))

        def body(t, carry):
            stage(2 * t, 0)
            stage(2 * t + 1, 1)
            return carry

        lax.fori_loop(0, 4, body, 0)

    own_q.wait()

    def q_arrived(i):
        @pl.when(i < 7)
        def _():
            n = source(i)
            drain(qb.at[n], qr.at[n])

    def keep_near(i, p, slot, acc):
        va[p] = acc
        vm[p] = m_ref[slot]

    unit_loop(NEAR, q_arrived, lambda n, m: m, keep_near)

    for k in range(NPIECE):
        landed(2, k)
    table_wait()

    def finish(i, p, slot, acc):
        f = jnp.exp2(vm[p] - m_ref[slot])
        acc = acc + va[p] * jnp.concatenate([f, f], axis=1)
        o = (acc[:, :DH] / acc[:, DH:]).astype(jnp.bfloat16)
        for t in range(HPG):
            ob[p, :, t * DH:(t + 1) * DH] = o[t * ROWS:(t + 1) * ROWS]

        @pl.when(i < 7)
        def _():
            out_copy(p).start()

    unit_loop(REST, lambda i: None, lambda n, m: jnp.maximum(m, vm[n]), finish)

    own_o = pltpu.make_async_copy(
        ob.at[h], out_hbm.at[:, pl.ds(pl.multiple_of(h * WIDTH, WIDTH), WIDTH)], loc.at[5])
    own_o.start()

    for i in range(7):
        t = target(i)
        for cp in kv_copies(i):
            cp.wait_send()
        q_copy(i).wait_send()
    for n, cond, d in (
        (0, z < 3, 0), (1, z == 0, 0), (2, x < 3, 0), (3, back & (z > 0), 4),
        (4, back & (z == 3), 4), (5, middle, 1), (6, back & middle, 3),
    ):
        @pl.when(cond)
        def _():
            drain(slab(d), bs.at[n])

    for n in range(4):
        @pl.when((x < 3) & (n != x))
        def _():
            drain(rb.at[0], sxs.at[n])

        @pl.when(n != z)
        def _():
            drain(ch, szs.at[n])
            drain(ch, gzs.at[n])

        if n > 0:
            @pl.when(n != x)
            def _():
                drain(rb.at[0], gxs.at[n])
    for i in range(7):
        p = source(i)
        drain(ob.at[p], os_.at[p])
        drain(out_hbm.at[:, pl.ds(pl.multiple_of(p * WIDTH, WIDTH), WIDTH)], or_.at[p])
    own_o.wait()


def per_device(queries, keys, values, vert_blocks):
    anywhere = pl.BlockSpec(memory_space=pl.ANY)
    queries, keys, values, vert_blocks = (
        pltpu.with_memory_space_constraint(e, pltpu.HBM)
        for e in (queries, keys, values, vert_blocks))
    dma = pltpu.SemaphoreType.DMA
    bf = jnp.bfloat16
    return pl.pallas_call(
        kernel,
        out_shape=jax.ShapeDtypeStruct((ROWS, NH * WIDTH), bf),
        in_specs=[anywhere, anywhere, anywhere, pl.BlockSpec(memory_space=pltpu.SMEM)],
        out_specs=anywhere,
        scratch_shapes=[
            pltpu.VMEM((NH, ROWS, WIDTH), bf),
            pltpu.VMEM((NEARROWS, 2 * DH), bf),
            pltpu.VMEM((MIDK, 2 * DH), bf),
            pltpu.VMEM((NVB * VW, 2 * DH), bf),
            pltpu.VMEM((NVB * VW, 2 * DH), bf),
            pltpu.VMEM((3, QUART, 2 * DH), bf),
            pltpu.VMEM((QUART, 2 * DH), bf),
            pltpu.VMEM((4, ROWS, 2 * DH), bf),
            pltpu.VMEM((ROWS, 2 * DH), bf),
            pltpu.VMEM((NH, ROWS, WIDTH), bf),
            pltpu.VMEM((2, M, RESTK), jnp.float32),
            pltpu.VMEM((2, M, VW), jnp.float32),
            pltpu.VMEM((NH, M, 2 * DH), jnp.float32),
            pltpu.VMEM((NH, M, VW), jnp.float32),
            dma((8,)), dma((NH,)), dma((NH,)), dma((NH,)), dma((NH,)),
            dma((8,)), dma((4, NPIECE)), *[dma((4,)) for _ in range(8)], dma((NH,)), dma((NH,)),
            pltpu.SemaphoreType.REGULAR((4,)), pltpu.SemaphoreType.REGULAR((4,)),
        ],
        compiler_params=pltpu.CompilerParams(
            collective_id=0, has_side_effects=True, vmem_limit_bytes=32 * 2**20),
        name="sparse_attention",
    )(queries, keys, values, vert_blocks)


def solution(mesh):
    placed = (
        P(("ctx", "head"), None),
        P(("ctx", "head"), None),
        P(("ctx", "head"), None),
        P("head", None),
    )
    return jax.shard_map(
        per_device, mesh=mesh, in_specs=placed, out_specs=P(("ctx", "head"), None), check_vma=False
    )
```
